128 devices in a mesh: feat: 64 (over x, y, z_lo, core), rows: 2 (over z_hi).
Axes of the slice: x: 4, y: 4, z: 4 (z_hi: 2, z_lo: 2; z = z_hi * 2 + z_lo), core: 2. Of those that a mesh axis runs over, the one named last changes fastest.
Arguments:
- embeddings: bfloat16 [256, 512], P('rows'), may hold values from -6 to 6
- sign_flips: float32 [524288], P('feat'), may hold values from -1 to 1, as said below
- gaussian: float32 [524288], P('feat'), may hold values from -5 to 5
- scales: float32 [524288], P('feat'), may hold values from 0.5 to 2
- phases: float32 [524288], P('feat'), may hold values from 0 to 6.2831855
- source_blocks: int32 [4096], P('feat'), may hold values from 0 to 4095, as said below
- block_permutations: bfloat16 [4096, 128, 128], P('feat'), may hold values from 0 to 1, as said below
- weights: float32 [524288], P('feat'), may hold values from -6 to 6
- targets: float32 [256], P('rows'), may hold values from -6 to 6
Outputs:
- predictions: float32 [256], P('rows')
- feature_grad: float32 [524288], P(('feat', 'rows'))
The draws below stay inside these ranges and needn't reach their ends.
Inputs may be any that keep to these rules, and one draw needn't show every extreme that they name: `sign_flips`: each entry is -1 or 1. `source_blocks`: A permutation of the 4096 block numbers. The 64 entries of each aligned run of 64 entries name exactly 1 block from every aligned run of 64 blocks. Each block_permutations[b] is a permutation matrix.
All inputs are finite; a program needn't handle non-finite values.
Results may differ from the reference program's by a relative error of at most 0.0003.
Values sent between devices are 32-bit elements; how exact they have to be, the bound alone decides.
A program may use at most 64 MiB of HBM per device.

```python
import math
import jax
import jax.numpy as jnp
from jax import lax

D = 512
FEATURE_COUNT = 524288
BLOCK = 128
ROWS = 256
BLOCKS = 4096
BLK_DEV = 64
FEAT_SHARDS = 64


def draw_sign_flips(key, part):
    return jax.random.rademacher(jax.random.fold_in(key, 11), (FEATURE_COUNT,), dtype=jnp.float32)


def draw_source_blocks(key, part):
    device_shards = FEAT_SHARDS
    local_count = BLK_DEV
    primary_key = jax.random.fold_in(key, 21)
    second_key = jax.random.fold_in(key, 22)
    dest_perm = jax.vmap(lambda k: jax.random.permutation(k, local_count))(jax.random.split(primary_key, device_shards))
    source_perm = jax.vmap(lambda k: jax.random.permutation(k, local_count))(jax.random.split(second_key, device_shards))
    target_index = jnp.arange(device_shards, dtype=jnp.int32)[:, None]
    quotient = dest_perm // device_shards
    remainder = dest_perm % device_shards
    source_dev = (target_index + remainder) % device_shards
    source_local = source_perm[source_dev, quotient * device_shards + remainder]
    table = source_dev * local_count + source_local
    return table.reshape(-1).astype(jnp.int32)


def draw_block_permutations(key, part):
    keys = jax.random.split(jax.random.fold_in(key, 31), BLOCKS)
    orders = jax.vmap(lambda k: jax.random.permutation(k, BLOCK))(keys)
    return jax.nn.one_hot(orders, BLOCK, dtype=jnp.float32).astype(jnp.bfloat16)


def shard_levels(rng, shape, pieces, smallest, largest):
    gain = 1.0
    for dim, blocks in pieces:
        heights = jax.random.uniform(jax.random.fold_in(jax.random.fold_in(rng, 6), dim), (blocks,), jnp.float32, smallest / len(pieces), largest / len(pieces))
        gain = gain * jnp.repeat(jnp.exp(heights), shape[dim] // blocks).reshape((-1,) + (1,) * (len(shape) - 1 - dim))
    return gain


def scatter_about(rng, dims, scale, bound, cuts=(), held_as=jnp.bfloat16):
    values = jax.random.normal(rng, dims, jnp.float32) * scale
    if len(cuts) > 0:
        values = shard_levels(rng, dims, cuts, -0.22, 0.18) * values
    return jnp.clip(values, min=-bound, max=bound).astype(held_as)


def setup_inputs(seed: int = 0) -> dict:
    streams_of = jax.random.split(jax.random.key(seed), 10)
    return {
        "embeddings": scatter_about(streams_of[0], (ROWS, D), 1.0, 6.0, ((0, 2),)),
        "sign_flips": draw_sign_flips(jax.random.fold_in(streams_of[9], 71), 0),
        "gaussian": scatter_about(streams_of[2], (FEATURE_COUNT,), 1.0, 5.0, ((0, 64),), jnp.float32),
        "scales": jnp.clip(jnp.exp(math.log(2.0) - 1.3862944 * jax.random.uniform(streams_of[3], (FEATURE_COUNT,), jnp.float32) ** shard_levels(streams_of[3], (FEATURE_COUNT,), ((0, 64),), -0.2, 0.2)), 0.5, 2.0),
        "phases": jnp.clip(6.2831855 * jax.random.uniform(streams_of[4], (FEATURE_COUNT,), jnp.float32) ** shard_levels(streams_of[4], (FEATURE_COUNT,), ((0, 64),), -0.2, 0.2), 0.0, 6.2831855),
        "source_blocks": draw_source_blocks(jax.random.fold_in(streams_of[9], 71), 0),
        "block_permutations": draw_block_permutations(jax.random.fold_in(streams_of[9], 71), 0),
        "weights": scatter_about(streams_of[7], (FEATURE_COUNT,), 1.0, 6.0, ((0, 64),), jnp.float32),
        "targets": scatter_about(streams_of[8], (ROWS,), 1.0, 6.0, ((0, 2),), jnp.float32),
    }


def walsh(field):
    row_count = field.shape[0]
    length = field.shape[1]
    butterfly_half_width = 1
    while butterfly_half_width < length:
        shaped = field.reshape(row_count, length // (2 * butterfly_half_width), 2, butterfly_half_width)
        upper_half = shaped[:, :, 0, :]
        lower_half = shaped[:, :, 1, :]
        field = jnp.stack([upper_half + lower_half, upper_half - lower_half], axis=2).reshape(row_count, length)
        butterfly_half_width = butterfly_half_width * 2
    return field * (1.0 / math.sqrt(FEATURE_COUNT))

def reference(embeddings, sign_flips, gaussian, scales, phases, source_blocks, block_permutations, weights, targets):
    tiled = jnp.tile(embeddings.astype(jnp.float32), (1, FEATURE_COUNT // D)) * sign_flips[None, :]
    first = walsh(tiled)
    picked = jnp.take(first.reshape(ROWS, BLOCKS, BLOCK), source_blocks, axis=1)
    mixed = jnp.einsum('rbj,bij->rbi', picked, block_permutations.astype(jnp.float32), precision=lax.Precision.HIGHEST)
    mixed = mixed.reshape(ROWS, FEATURE_COUNT) * gaussian[None, :]
    second = walsh(mixed)
    features = jnp.cos(scales[None, :] * second + phases[None, :])
    predictions = jnp.dot(features, weights, precision=lax.Precision.HIGHEST) * (1.0 / math.sqrt(FEATURE_COUNT))
    residual = predictions - targets
    feature_grad = jnp.dot(residual, features, precision=lax.Precision.HIGHEST) * (1.0 / math.sqrt(ROWS))
    return (predictions, feature_grad)
```

```python
import functools
import math

import jax
import jax.numpy as jnp
from jax import lax
from jax.experimental import pallas as pl
from jax.experimental.pallas import tpu as pltpu
from jax.sharding import PartitionSpec as P

FEATURE_COUNT = 524288
LANES = 128
N_BLOCKS = 4096
F32 = jnp.float32
BF16 = jnp.bfloat16


def signs_128():
    i = lax.broadcasted_iota(jnp.int32, (LANES, LANES), 0)
    j = lax.broadcasted_iota(jnp.int32, (LANES, LANES), 1)
    v = jnp.bitwise_and(i, j)
    v = jnp.bitwise_xor(v, jnp.right_shift(v, 4))
    v = jnp.bitwise_xor(v, jnp.right_shift(v, 2))
    v = jnp.bitwise_xor(v, jnp.right_shift(v, 1))
    return (1 - 2 * jnp.bitwise_and(v, 1)).astype(F32).astype(BF16)


def pieces(x):
    a = x.astype(BF16)
    rest = x - a.astype(F32)
    b = rest.astype(BF16)
    c = (rest - b.astype(F32)).astype(BF16)
    return a, b, c


def times_h(x, h2, h1):
    a, b, c = pieces(x)
    ab = jnp.concatenate([a, b], axis=1)
    return jnp.dot(ab, h2, preferred_element_type=F32) + jnp.dot(
        c, h1, preferred_element_type=F32
    )


def h_times(x, h2, h1):
    a, b, c = pieces(x)
    ab = jnp.concatenate([a, b], axis=0)
    return jnp.dot(h2, ab, preferred_element_type=F32) + jnp.dot(
        h1, c, preferred_element_type=F32
    )


def butterfly(values):
    n = len(values)
    half = 1
    values = list(values)
    while half < n:
        out = [None] * n
        for base in range(0, n, 2 * half):
            for k in range(half):
                u, v = values[base + k], values[base + half + k]
                out[base + k] = u + v
                out[base + half + k] = u - v
        values = out
        half *= 2
    return values


TWO_PI_A = 6.28125
TWO_PI_B = 2.0 * math.pi - 6.28125


def cos_coefficients():
    import numpy as np

    n = 7
    k = np.arange(n)
    u = 0.5 * math.pi**2 * (1.0 + np.cos((k + 0.5) * math.pi / n)) * 1.01
    v = np.stack([u**p for p in range(n)], axis=1)
    c = np.linalg.solve(v, np.cos(np.sqrt(u)))
    return [float(x) for x in c]


COS = cos_coefficients()


def cosine(x):
    n = jnp.round(x * (1.0 / (2.0 * math.pi)))
    r = (x - n * TWO_PI_A) - n * TWO_PI_B
    u = r * r
    acc = COS[-1] * u + COS[-2]
    for c in COS[-3::-1]:
        acc = acc * u + c
    return acc


def head_kernel(
    places_ref, targets_ref, emb_ref, gathered_ref, grad_ref, pred_ref,
    emb32, part, first, placed, feats,
):
    me = lax.axis_index("feat")
    h1 = signs_128()
    h2r = jnp.concatenate([h1, h1], axis=0)
    h2l = jnp.concatenate([h1, h1], axis=1)
    for d in range(4):
        emb32[d] = emb_ref[:, d * LANES : (d + 1) * LANES].astype(F32)
    emb = [
        [emb32[d, pl.ds(2 * me + r, 1), :] for d in range(4)]
        for r in range(2)
    ]

    for k_hi in range(8):
        for d in range(4):
            s = gathered_ref[0, pl.ds(512 * k_hi + d, LANES, stride=4), :]
            part[k_hi, d] = jnp.dot(h1, s.astype(BF16), preferred_element_type=F32)

    def stage_u(t, _):
        rows = pl.ds(pl.multiple_of(8 * t, 8), 8)
        cols = []
        for d in range(4):
            cols.append(butterfly([part[k, d, rows, :] for k in range(8)]))
        for k in range(8):
            for r in range(2):
                u = butterfly([emb[r][d] * cols[d][k] for d in range(4)])
                for c in range(4):
                    placed[r, pl.ds(pl.multiple_of(1024 * c + 128 * k + 8 * t, 8), 8), :] = u[c]
        return 0

    lax.fori_loop(0, 16, stage_u, 0)

    for r in range(2):

        def stage_f(t, _, r=r):
            rows = pl.ds(pl.multiple_of(256 * t, 256), 256)
            first[r, rows, :] = times_h(placed[r, rows, :], h2r, h1)
            return 0

        lax.fori_loop(0, 16, stage_f, 0)

    def stage_g(t, _):
        for q in range(16):
            b = 16 * t + q
            s = places_ref[b]
            for r in range(2):
                placed[r, pl.ds(b, 1), :] = first[r, pl.ds(s, 1), :]
        return 0

    lax.fori_loop(0, N_BLOCKS // 16, stage_g, 0)

    def stage_m(t, _):
        xs = [[], []]
        for q in range(16):
            rows = pl.ds(pl.multiple_of(128 * t + 8 * q, 8), 8)
            order = gathered_ref[1, rows, :].astype(jnp.int32)
            g = gathered_ref[2, rows, :]
            for r in range(2):
                x = placed[r, rows, :]
                xs[r].append(jnp.take_along_axis(x, order, axis=1) * g)
        rows = pl.ds(pl.multiple_of(128 * t, 128), 128)
        for r in range(2):
            x = jnp.concatenate(xs[r], axis=0)
            first[r, rows, :] = h_times(times_h(x, h2r, h1), h2l, h1)
        return 0

    lax.fori_loop(0, 32, stage_m, 0)

    def stage_c(t, acc):
        out = []
        for r in range(2):
            row = [pl.ds(pl.multiple_of(128 * k + 8 * t, 8), 8) for k in range(32)]
            y = butterfly([first[r, row[k], :] for k in range(32)])
            total = acc[r]
            for k in range(32):
                scale = gathered_ref[3, row[k], :] * (1.0 / FEATURE_COUNT)
                f = cosine(scale * y[k] + gathered_ref[4, row[k], :])
                feats[r, row[k], :] = f
                total = total + f * gathered_ref[5, row[k], :]
            out.append(total)
        return tuple(out)

    zero = jnp.zeros((8, LANES), F32)
    acc = lax.fori_loop(0, 16, stage_c, (zero, zero))
    residual = []
    for r in range(2):
        p = jnp.sum(acc[r], axis=(0, 1), keepdims=True) * (1.0 / math.sqrt(FEATURE_COUNT))
        pred_ref[r] = jnp.broadcast_to(p, (8, LANES))
        residual.append((p - targets_ref[2 * me + r]) * (1.0 / 16.0))

    def stage_r(t, _):
        rows = pl.ds(pl.multiple_of(64 * t, 64), 64)
        grad_ref[rows, :] = feats[0, rows, :] * residual[0] + feats[1, rows, :] * residual[1]
        return 0

    lax.fori_loop(0, 64, stage_r, 0)


def local(
    embeddings,
    sign_flips,
    gaussian,
    scales,
    phases,
    source_blocks,
    block_permutations,
    weights,
    targets,
):
    order = jnp.einsum(
        "bij,j->bi", block_permutations, jnp.arange(LANES, dtype=BF16),
        preferred_element_type=F32,
    )
    rows = lambda v: v.reshape(-1, LANES)
    packed = jnp.stack(
        [rows(sign_flips), order, rows(gaussian), rows(scales), rows(phases), rows(weights)]
    )
    gathered = lax.all_gather(packed, "feat", axis=1, tiled=True)
    places = lax.all_gather((source_blocks % 4) * 1024 + source_blocks // 4, "feat", tiled=True)
    vmem = pl.BlockSpec(memory_space=pltpu.VMEM)
    smem = pl.BlockSpec(memory_space=pltpu.SMEM)
    field = pltpu.VMEM((2, N_BLOCKS, LANES), F32)
    grads, preds = pl.pallas_call(
        head_kernel,
        out_shape=(
            jax.ShapeDtypeStruct((N_BLOCKS, LANES), F32),
            jax.ShapeDtypeStruct((2, 8, LANES), F32),
        ),
        in_specs=[smem, smem, vmem, vmem],
        out_specs=(vmem, vmem),
        scratch_shapes=[
            pltpu.VMEM((4, 128, LANES), F32),
            pltpu.VMEM((8, 4, LANES, LANES), F32),
            field, field, field,
        ],
        compiler_params=pltpu.CompilerParams(vmem_limit_bytes=60 * 2**20),
    )(places, targets, embeddings, gathered)
    predictions = lax.all_gather(preds[:, 0, 0], "feat", tiled=True)
    feature_grad = lax.psum_scatter(
        grads.reshape(-1), ("feat", "rows"), scatter_dimension=0, tiled=True
    )
    return predictions, feature_grad


def solution(mesh):
    in_specs = (
        P("rows", None), P("feat"), P("feat"), P("feat"), P("feat"), P("feat"),
        P("feat", None, None), P("feat"), P("rows"),
    )
    out_specs = (P("rows"), P(("feat", "rows")))
    return jax.shard_map(local, mesh=mesh, in_specs=in_specs, out_specs=out_specs, check_vma=False)
```

```python
import functools
import math

import jax
import jax.numpy as jnp
from jax import lax
from jax.experimental import pallas as pl
from jax.experimental.pallas import tpu as pltpu
from jax.sharding import PartitionSpec as P

FEATURE_COUNT = 524288
LANES = 128
N_BLOCKS = 4096
F32 = jnp.float32
BF16 = jnp.bfloat16


def signs_128():
    i = lax.broadcasted_iota(jnp.int32, (LANES, LANES), 0)
    j = lax.broadcasted_iota(jnp.int32, (LANES, LANES), 1)
    v = jnp.bitwise_and(i, j)
    v = jnp.bitwise_xor(v, jnp.right_shift(v, 4))
    v = jnp.bitwise_xor(v, jnp.right_shift(v, 2))
    v = jnp.bitwise_xor(v, jnp.right_shift(v, 1))
    return (1 - 2 * jnp.bitwise_and(v, 1)).astype(F32).astype(BF16)


def pieces(x):
    a = x.astype(BF16)
    rest = x - a.astype(F32)
    b = rest.astype(BF16)
    c = (rest - b.astype(F32)).astype(BF16)
    return a, b, c


def times_h(x, h2, h1):
    a, b, c = pieces(x)
    ab = jnp.concatenate([a, b], axis=1)
    return jnp.dot(ab, h2, preferred_element_type=F32) + jnp.dot(
        c, h1, preferred_element_type=F32
    )


def h_times(x, h2, h1):
    a, b, c = pieces(x)
    ab = jnp.concatenate([a, b], axis=0)
    return jnp.dot(h2, ab, preferred_element_type=F32) + jnp.dot(
        h1, c, preferred_element_type=F32
    )


def butterfly(values):
    n = len(values)
    half = 1
    values = list(values)
    while half < n:
        out = [None] * n
        for base in range(0, n, 2 * half):
            for k in range(half):
                u, v = values[base + k], values[base + half + k]
                out[base + k] = u + v
                out[base + half + k] = u - v
        values = out
        half *= 2
    return values


TWO_PI_A = 6.28125
TWO_PI_B = 2.0 * math.pi - 6.28125


def cos_coefficients():
    import numpy as np

    n = 7
    k = np.arange(n)
    u = 0.5 * math.pi**2 * (1.0 + np.cos((k + 0.5) * math.pi / n)) * 1.01
    v = np.stack([u**p for p in range(n)], axis=1)
    c = np.linalg.solve(v, np.cos(np.sqrt(u)))
    return [float(x) for x in c]


COS = cos_coefficients()


def cosine(x):
    n = jnp.round(x * (1.0 / (2.0 * math.pi)))
    r = (x - n * TWO_PI_A) - n * TWO_PI_B
    u = r * r
    acc = COS[-1] * u + COS[-2]
    for c in COS[-3::-1]:
        acc = acc * u + c
    return acc


MESH = pl.DeviceIdType.MESH
ALL = slice(None)
ORDERS = ("zyx", "zxy", "yxz", "xyz")
STREAM_SEMS = 16


class Place:
    def __init__(self):
        me = lax.axis_index("feat")
        self.h = lax.axis_index("rows")
        self.c = lax.rem(me, 2)
        self.z = lax.rem(me // 2, 2)
        self.y = lax.rem(me // 4, 4)
        self.x = me // 16
        self.zz = 2 * self.h + self.z

    def at(self, x=None, y=None, z=None, c=None, h=None):
        x = self.x if x is None else x
        y = self.y if y is None else y
        z = self.z if z is None else z
        c = self.c if c is None else c
        h = self.h if h is None else h
        return (((x * 4 + y) * 2 + z) * 2 + c, h)

    def along(self, dim, step):
        a = lax.rem(getattr(self, dim) + 4 + step, 4)
        if dim == "zz":
            return self.at(z=lax.rem(a, 2), h=a // 2)
        return self.at(**{dim: a})

    def neighbours(self):
        out = [self.along(d, s) for d in ("x", "y", "zz") for s in (1, -1)]
        return out + [self.at(c=1 - self.c), self.along("zz", 2)]


def greet(place):
    barrier = pltpu.get_barrier_semaphore()
    others = place.neighbours()
    for device in others:
        pl.semaphore_signal(barrier, inc=1, device_id=device, device_id_type=MESH)
    pl.semaphore_wait(barrier, len(others))


class Sender:
    def __init__(self, send, recv):
        self.send, self.recv = send, recv
        self.started = []

    def copy(self, ref, dst, sem, device):
        return pltpu.make_async_remote_copy(
            src_ref=ref, dst_ref=dst, send_sem=self.send.at[sem], recv_sem=self.recv.at[sem],
            device_id=device, device_id_type=MESH,
        )

    def start(self, ref, dst, sem, device):
        copy = self.copy(ref, dst, sem, device)
        copy.start()
        self.started.append(copy)

    def arrived(self, ref, sem, device):
        self.copy(ref, ref, sem, device).wait_recv()

    def finish(self):
        for copy in self.started:
            copy.wait_send()


def gather_stream(place, sender, base, order, get, halves):
    sel = {"x": place.x, "y": place.y, "z": place.z, "c": place.c}
    partner = place.at(c=1 - place.c)
    sem = base
    mirrored = []

    def mirror(index, **where):
        here = get({**sel, **where}, None)
        sender.start(here, here, index, partner)
        mirrored.append((get({**sel, **where, "c": 1 - place.c}, None), index))

    last = len(order) - 1
    for phase, dim in enumerate(order):
        final = phase == last
        if dim == "z":
            other = 1 - place.z
            ways = ((0, place.h), (1, 1 - place.h)) if halves else ((None, place.h),)
            for k, (half, h) in enumerate(ways):
                ref = get(sel, half)
                sender.start(ref, ref, sem + k, place.at(z=other, h=h))
            if final:
                mirror(base + 12)
            yield
            for k, (half, h) in enumerate(ways):
                sender.arrived(get({**sel, "z": other}, half), sem + k, place.at(z=other, h=h))
            if final:
                mirror(base + 13, z=other)
            sem += 2
        else:
            a = sel[dim]
            up, down = place.along(dim, 1), place.along(dim, -1)
            above, below = lax.rem(a + 1, 4), lax.rem(a + 3, 4)
            across = lax.rem(a + 2, 4)
            own = get(sel, None)
            sender.start(own, own, sem, up)
            sender.start(own, own, sem + 1, down)
            if final:
                mirror(base + 12)
            yield
            sender.arrived(get({**sel, dim: below}, None), sem, down)
            ref = get({**sel, dim: below}, 0 if halves else None)
            sender.start(ref, ref, sem + 2, up)
            sender.arrived(get({**sel, dim: above}, None), sem + 1, up)
            if halves:
                ref = get({**sel, dim: above}, 1)
                sender.start(ref, ref, sem + 3, down)
            if final:
                mirror(base + 13, **{dim: below})
                mirror(base + 14, **{dim: above})
            yield
            sender.arrived(get({**sel, dim: across}, 0 if halves else None), sem + 2, down)
            if halves:
                sender.arrived(get({**sel, dim: across}, 1), sem + 3, up)
            if final:
                mirror(base + 15, **{dim: across})
            sem += 4
        sel[dim] = ALL
    yield
    for ref, index in mirrored:
        sender.arrived(ref, index, partner)


def run_streams(streams):
    live = list(streams)
    while live:
        left = []
        for s in live:
            try:
                next(s)
                left.append(s)
            except StopIteration:
                pass
        live = left


GROUPS = ((0, 1), (1, 3), (3, 6))


def gather_kernel(
    sources_ref, signs_ref, gaussian_ref, scales_ref, phases_ref, weights_ref, perms_ref,
    out_ref, places_ref,
    perms, send, recv, own,
):
    place = Place()
    x, y, z, c = place.x, place.y, place.z, place.c
    given = [signs_ref, None, gaussian_ref, scales_ref, phases_ref, weights_ref]
    copies = [pltpu.make_async_copy(perms_ref, perms, own.at[6])]
    for v, ref in enumerate(given):
        if ref is not None:
            copies.append(pltpu.make_async_copy(ref, out_ref.at[v, x, y, z, c], own.at[v]))
    copies.append(pltpu.make_async_copy(sources_ref, places_ref.at[x, y, z, c], own.at[7]))
    for copy in copies:
        copy.start()
    greet(place)
    for copy in copies:
        copy.wait()
    sender = Sender(send, recv)

    def getter(group, part):
        vs = slice(*GROUPS[group])

        def get(sel, half):
            rows = pl.ds(16 * part, 16) if half is None else pl.ds(16 * part + 8 * half, 8)
            return out_ref.at[vs, sel["x"], sel["y"], sel["z"], sel["c"], rows, :]

        return get

    def get_places(sel, half):
        return places_ref.at[sel["x"], sel["y"], sel["z"], sel["c"]]

    streams = []
    for group in range(3):
        for part in range(4):
            base = STREAM_SEMS * (4 * group + part)
            streams.append(
                gather_stream(place, sender, base, ORDERS[part], getter(group, part), True)
            )
    streams.append(gather_stream(place, sender, STREAM_SEMS * 12, "zyx", get_places, False))
    for s in streams[:4]:
        next(s)
    lanes = lax.broadcasted_iota(jnp.int32, (8, LANES), 1).astype(F32).astype(BF16)

    def order_of(t, _):
        rows = []
        for q in range(8):
            line = lax.dot_general(
                lanes, perms[8 * t + q], (((1,), (1,)), ((), ())), preferred_element_type=F32
            )
            rows.append(line[0:1])
        out_ref[1, x, y, z, c, pl.ds(pl.multiple_of(8 * t, 8), 8), :] = jnp.concatenate(rows, axis=0)
        return 0

    lax.fori_loop(0, 8, order_of, 0)
    for s in streams[4:]:
        next(s)
    run_streams(streams)
    sender.finish()


DIMS = ("x", "y", "zz")
REDUCE_ORDERS = (("x", "y", "zz"), ("y", "zz", "x"), ("zz", "x", "y"), ("zz", "y", "x"))


def reduce_scratch():
    out = []
    for first, second, _ in REDUCE_ORDERS:
        wide = [d for d in DIMS if d != first]
        half = tuple(2 if d == second else 4 for d in wide)
        for shape in (half, half, (4, 4), (4, 4), (2,), (2,), (4,), (4,)):
            out.append(pltpu.VMEM(shape + (8, LANES), F32))
    return out


def reduce_part(place, sender, base, p, order, total, slots, last, out_ref):
    where = {d: None for d in DIMS}

    def cut(dim, index, rest=None, side=None):
        parts = []
        for d in DIMS:
            if d == dim:
                parts.append(index)
            elif where[d] is not None:
                parts.append(where[d])
            elif d == rest:
                parts.append(pl.ds(2 * side, 2))
            else:
                parts.append(ALL)
        return (p, *parts)

    for phase, dim in enumerate(order):
        a = getattr(place, dim)
        up, down = place.along(dim, 1), place.along(dim, -1)
        above, below, across = lax.rem(a + 1, 4), lax.rem(a + 3, 4), lax.rem(a + 2, 4)
        sem = base + 4 * phase
        if phase < 2:
            rest = order[phase + 1]
            half_up, half_down, whole_up, whole_down = slots[4 * phase : 4 * phase + 4]
            sender.start(total.at[cut(dim, across, rest, 0)], half_up, sem, up)
            sender.start(total.at[cut(dim, across, rest, 1)], half_down, sem + 1, down)
            yield
            sender.arrived(half_up, sem, down)
            i = cut(dim, above, rest, 0)
            total[i] = total[i] + half_up[...]
            sender.start(total.at[cut(dim, above)], whole_up, sem + 2, up)
            sender.arrived(half_down, sem + 1, up)
            i = cut(dim, below, rest, 1)
            total[i] = total[i] + half_down[...]
            sender.start(total.at[cut(dim, below)], whole_down, sem + 3, down)
            yield
            sender.arrived(whole_up, sem + 2, down)
            sender.arrived(whole_down, sem + 3, up)
            i = cut(dim, a)
            total[i] = total[i] + (whole_up[...] + whole_down[...])
        else:
            far = place.along(dim, 2)
            sender.start(total.at[cut(dim, above)], last.at[p, 0], sem, up)
            sender.start(total.at[cut(dim, below)], last.at[p, 1], sem + 1, down)
            sender.start(total.at[cut(dim, across)], last.at[p, 2], sem + 2, far)
            yield
            sender.arrived(last.at[p, 0], sem, down)
            sender.arrived(last.at[p, 1], sem + 1, up)
            sender.arrived(last.at[p, 2], sem + 2, far)
            out_ref[8 * p : 8 * p + 8, :] = total[cut(dim, a)] + (
                last[p, 0] + last[p, 1] + last[p, 2]
            )
        where[dim] = a


def reduce_kernel(
    grads_ref, preds_ref, out_ref, line_ref, theirs, total, last, lines, send, recv, *slots
):
    place = Place()
    x, y, z, c, h = place.x, place.y, place.z, place.c, place.h
    partner = place.at(c=1 - c)
    me = ((x * 4 + y) * 2 + z) * 2 + c
    lane = lax.broadcasted_iota(jnp.int32, (1, LANES), 1)
    lines[x, y, z, c] = jnp.where(
        lane == 2 * me, preds_ref[0, 0:1, :],
        jnp.where(lane == 2 * me + 1, preds_ref[1, 0:1, :], 0.0),
    )
    greet(place)
    sender = Sender(send, recv)
    for p in range(4):
        sender.start(grads_ref.at[:, :, :, 1 - c, :, p], theirs.at[p], 16 * p, partner)

    def get_lines(sel, half):
        return lines.at[sel["x"], sel["y"], sel["z"], sel["c"]]

    def part(p):
        sender.arrived(theirs.at[p], 16 * p, partner)
        for hh in range(2):
            for zed in range(2):
                total[p, :, :, 2 * hh + zed] = (
                    grads_ref[:, :, zed, c, hh, p] + theirs[p, :, :, zed, hh]
                )
        yield from reduce_part(
            place, sender, 16 * p + 1, p, REDUCE_ORDERS[p], total, slots[8 * p : 8 * p + 8],
            last, out_ref,
        )

    run_streams(
        [part(p) for p in range(4)]
        + [gather_stream(place, sender, 64, "zyx", get_lines, False)]
    )
    line = jnp.zeros((1, LANES), F32)
    for i in range(64):
        line = line + lines[i // 16, (i // 4) % 4, (i // 2) % 2, i % 2]
    line_ref[...] = line
    sender.finish()


def head_kernel(
    places_ref, targets_ref, emb_ref, gathered_ref, grad_ref, pred_ref,
    emb32, part, first, placed, feats,
):
    me = lax.axis_index("feat")
    h1 = signs_128()
    h2r = jnp.concatenate([h1, h1], axis=0)
    h2l = jnp.concatenate([h1, h1], axis=1)
    for d in range(4):
        emb32[d] = emb_ref[:, d * LANES : (d + 1) * LANES].astype(F32)
    emb = [
        [emb32[d, pl.ds(2 * me + r, 1), :] for d in range(4)]
        for r in range(2)
    ]

    for k_hi in range(8):
        for d in range(4):
            s = gathered_ref[0, pl.ds(512 * k_hi + d, LANES, stride=4), :]
            part[k_hi, d] = jnp.dot(h1, s.astype(BF16), preferred_element_type=F32)

    def stage_u(t, _):
        rows = pl.ds(pl.multiple_of(8 * t, 8), 8)
        cols = []
        for d in range(4):
            cols.append(butterfly([part[k, d, rows, :] for k in range(8)]))
        for k in range(8):
            for r in range(2):
                u = butterfly([emb[r][d] * cols[d][k] for d in range(4)])
                for c in range(4):
                    placed[r, pl.ds(pl.multiple_of(1024 * c + 128 * k + 8 * t, 8), 8), :] = u[c]
        return 0

    lax.fori_loop(0, 16, stage_u, 0)

    for r in range(2):

        def stage_f(t, _, r=r):
            rows = pl.ds(pl.multiple_of(256 * t, 256), 256)
            first[r, rows, :] = times_h(placed[r, rows, :], h2r, h1)
            return 0

        lax.fori_loop(0, 16, stage_f, 0)

    def stage_g(t, _):
        for q in range(16):
            b = 16 * t + q
            s = places_ref[b]
            for r in range(2):
                placed[r, pl.ds(b, 1), :] = first[r, pl.ds(s, 1), :]
        return 0

    lax.fori_loop(0, N_BLOCKS // 16, stage_g, 0)

    def stage_m(t, _):
        xs = [[], []]
        for q in range(16):
            rows = pl.ds(pl.multiple_of(128 * t + 8 * q, 8), 8)
            order = gathered_ref[1, rows, :].astype(jnp.int32)
            g = gathered_ref[2, rows, :]
            for r in range(2):
                x = placed[r, rows, :]
                xs[r].append(jnp.take_along_axis(x, order, axis=1) * g)
        rows = pl.ds(pl.multiple_of(128 * t, 128), 128)
        for r in range(2):
            x = jnp.concatenate(xs[r], axis=0)
            first[r, rows, :] = h_times(times_h(x, h2r, h1), h2l, h1)
        return 0

    lax.fori_loop(0, 32, stage_m, 0)

    def stage_c(t, acc):
        out = []
        for r in range(2):
            row = [pl.ds(pl.multiple_of(128 * k + 8 * t, 8), 8) for k in range(32)]
            y = butterfly([first[r, row[k], :] for k in range(32)])
            total = acc[r]
            for k in range(32):
                scale = gathered_ref[3, row[k], :] * (1.0 / FEATURE_COUNT)
                f = cosine(scale * y[k] + gathered_ref[4, row[k], :])
                feats[r, row[k], :] = f
                total = total + f * gathered_ref[5, row[k], :]
            out.append(total)
        return tuple(out)

    zero = jnp.zeros((8, LANES), F32)
    acc = lax.fori_loop(0, 16, stage_c, (zero, zero))
    residual = []
    for r in range(2):
        p = jnp.sum(acc[r], axis=(0, 1), keepdims=True) * (1.0 / math.sqrt(FEATURE_COUNT))
        pred_ref[r] = jnp.broadcast_to(p, (8, LANES))
        residual.append((p - targets_ref[2 * me + r]) * (1.0 / 16.0))

    def stage_r(t, _):
        rows = pl.ds(pl.multiple_of(64 * t, 64), 64)
        grad_ref[rows, :] = feats[0, rows, :] * residual[0] + feats[1, rows, :] * residual[1]
        return 0

    lax.fori_loop(0, 64, stage_r, 0)


def local(
    embeddings,
    sign_flips,
    gaussian,
    scales,
    phases,
    source_blocks,
    block_permutations,
    weights,
    targets,
):
    rows = lambda v: v.reshape(-1, LANES)
    vmem = pl.BlockSpec(memory_space=pltpu.VMEM)
    smem = pl.BlockSpec(memory_space=pltpu.SMEM)
    any_ = pl.BlockSpec(memory_space=pl.ANY)
    sources = jnp.pad(source_blocks, (0, 64)).reshape(1, LANES)
    gathered, sources_all = pl.pallas_call(
        gather_kernel,
        out_shape=(
            jax.ShapeDtypeStruct((6, 4, 4, 2, 2, 64, LANES), F32),
            jax.ShapeDtypeStruct((4, 4, 2, 2, 1, LANES), jnp.int32),
        ),
        in_specs=[vmem] + [any_] * 6,
        out_specs=(vmem, vmem),
        scratch_shapes=[
            pltpu.VMEM((64, LANES, LANES), BF16),
            pltpu.SemaphoreType.DMA((STREAM_SEMS * 13,)),
            pltpu.SemaphoreType.DMA((STREAM_SEMS * 13,)),
            pltpu.SemaphoreType.DMA((8,)),
        ],
        compiler_params=pltpu.CompilerParams(
            vmem_limit_bytes=40 * 2**20, collective_id=0, has_side_effects=True
        ),
    )(
        sources, rows(sign_flips), rows(gaussian), rows(scales), rows(phases), rows(weights),
        block_permutations,
    )
    gathered = gathered.reshape(6, N_BLOCKS, LANES)
    sources_all = sources_all.reshape(64, LANES)[:, :64].reshape(-1)
    places = (sources_all % 4) * 1024 + sources_all // 4
    field = pltpu.VMEM((2, N_BLOCKS, LANES), F32)
    grads, preds = pl.pallas_call(
        head_kernel,
        out_shape=(
            jax.ShapeDtypeStruct((N_BLOCKS, LANES), F32),
            jax.ShapeDtypeStruct((2, 8, LANES), F32),
        ),
        in_specs=[smem, smem, vmem, vmem],
        out_specs=(vmem, vmem),
        scratch_shapes=[
            pltpu.VMEM((4, 128, LANES), F32),
            pltpu.VMEM((8, 4, LANES, LANES), F32),
            field, field, field,
        ],
        compiler_params=pltpu.CompilerParams(vmem_limit_bytes=60 * 2**20),
    )(places, targets, embeddings, gathered)
    grad_out, line = pl.pallas_call(
        reduce_kernel,
        out_shape=(
            jax.ShapeDtypeStruct((32, LANES), F32),
            jax.ShapeDtypeStruct((1, LANES), F32),
        ),
        in_specs=[vmem, vmem],
        out_specs=(vmem, vmem),
        scratch_shapes=[
            pltpu.VMEM((4, 4, 4, 2, 2, 8, LANES), F32),
            pltpu.VMEM((4, 4, 4, 4, 8, LANES), F32),
            pltpu.VMEM((4, 3, 8, LANES), F32),
            pltpu.VMEM((4, 4, 2, 2, 1, LANES), F32),
            pltpu.SemaphoreType.DMA((80,)),
            pltpu.SemaphoreType.DMA((80,)),
            *reduce_scratch(),
        ],
        compiler_params=pltpu.CompilerParams(
            vmem_limit_bytes=40 * 2**20, collective_id=1, has_side_effects=True
        ),
    )(grads.reshape(4, 4, 2, 2, 2, 4, 8, LANES), preds)
    return line.reshape(-1), grad_out.reshape(-1)


def solution(mesh):
    in_specs = (
        P("rows", None), P("feat"), P("feat"), P("feat"), P("feat"), P("feat"),
        P("feat", None, None), P("feat"), P("rows"),
    )
    out_specs = (P("rows"), P(("feat", "rows")))
    return jax.shard_map(local, mesh=mesh, in_specs=in_specs, out_specs=out_specs, check_vma=False)
```

```python
import functools
import math

import jax
import jax.numpy as jnp
from jax import lax
from jax.experimental import pallas as pl
from jax.experimental.pallas import tpu as pltpu
from jax.sharding import PartitionSpec as P

FEATURE_COUNT = 524288
LANES = 128
N_BLOCKS = 4096
F32 = jnp.float32
BF16 = jnp.bfloat16


def signs_128():
    i = lax.broadcasted_iota(jnp.int32, (LANES, LANES), 0)
    j = lax.broadcasted_iota(jnp.int32, (LANES, LANES), 1)
    v = jnp.bitwise_and(i, j)
    v = jnp.bitwise_xor(v, jnp.right_shift(v, 4))
    v = jnp.bitwise_xor(v, jnp.right_shift(v, 2))
    v = jnp.bitwise_xor(v, jnp.right_shift(v, 1))
    return (1 - 2 * jnp.bitwise_and(v, 1)).astype(F32).astype(BF16)


def times_h(x, h2):
    a = x.astype(BF16)
    b = (x - a.astype(F32)).astype(BF16)
    return jnp.dot(jnp.concatenate([a, b], axis=1), h2, preferred_element_type=F32)


def butterfly(values):
    n = len(values)
    half = 1
    values = list(values)
    while half < n:
        out = [None] * n
        for base in range(0, n, 2 * half):
            for k in range(half):
                u, v = values[base + k], values[base + half + k]
                out[base + k] = u + v
                out[base + half + k] = u - v
        values = out
        half *= 2
    return values


TWO_PI_A = 6.28125
TWO_PI_B = 2.0 * math.pi - 6.28125


def cos_coefficients():
    import numpy as np

    n = 7
    k = np.arange(n)
    u = 0.5 * math.pi**2 * (1.0 + np.cos((k + 0.5) * math.pi / n)) * 1.01
    v = np.stack([u**p for p in range(n)], axis=1)
    c = np.linalg.solve(v, np.cos(np.sqrt(u)))
    return [float(x) for x in c]


COS = cos_coefficients()


def cosine(x):
    n = jnp.round(x * (1.0 / (2.0 * math.pi)))
    r = (x - n * TWO_PI_A) - n * TWO_PI_B
    u = r * r
    acc = COS[-1] * u + COS[-2]
    for c in COS[-3::-1]:
        acc = acc * u + c
    return acc


MESH = pl.DeviceIdType.MESH
ALL = slice(None)
ORDERS = ("zyx", "zxy", "yxz", "xyz")
STREAM_SEMS = 14
DIMS = ("x", "y", "zz")


class Place:
    def __init__(self):
        me = lax.axis_index("feat")
        self.h = lax.axis_index("rows")
        self.c = lax.rem(me, 2)
        self.z = lax.rem(me // 2, 2)
        self.y = lax.rem(me // 4, 4)
        self.x = me // 16
        self.zz = 2 * self.h + self.z

    def at(self, x=None, y=None, z=None, c=None, h=None):
        x = self.x if x is None else x
        y = self.y if y is None else y
        z = self.z if z is None else z
        c = self.c if c is None else c
        h = self.h if h is None else h
        return (((x * 4 + y) * 2 + z) * 2 + c, h)

    def along(self, dim, step):
        a = lax.rem(getattr(self, dim) + 4 + step, 4)
        if dim == "zz":
            return self.at(z=lax.rem(a, 2), h=a // 2)
        return self.at(**{dim: a})

    def neighbours(self):
        out = [self.along(d, s) for d in DIMS for s in (1, -1, 2)]
        return out + [self.at(c=1 - self.c)]


def greet(place):
    barrier = pltpu.get_barrier_semaphore()
    others = place.neighbours()
    for device in others:
        pl.semaphore_signal(barrier, inc=1, device_id=device, device_id_type=MESH)
    pl.semaphore_wait(barrier, len(others))


class Sender:
    def __init__(self, send, recv):
        self.send, self.recv = send, recv
        self.started = []

    def copy(self, ref, dst, sem, device):
        return pltpu.make_async_remote_copy(
            src_ref=ref, dst_ref=dst, send_sem=self.send.at[sem], recv_sem=self.recv.at[sem],
            device_id=device, device_id_type=MESH,
        )

    def start(self, ref, dst, sem, device):
        copy = self.copy(ref, dst, sem, device)
        copy.start()
        self.started.append(copy)

    def arrived(self, ref, sem, device):
        self.copy(ref, ref, sem, device).wait_recv()

    def finish(self):
        for copy in self.started:
            copy.wait_send()


def gather_stream(place, sender, base, order, get, halves):
    sel = {"x": place.x, "y": place.y, "z": place.z, "c": place.c}
    partner = place.at(c=1 - place.c)
    sem = base
    mirrored = []

    def mirror(index, **where):
        here = get({**sel, **where}, None)
        sender.start(here, here, index, partner)
        mirrored.append((get({**sel, **where, "c": 1 - place.c}, None), index))

    for phase, dim in enumerate(order):
        final = phase == 2
        if dim == "z":
            other = 1 - place.z
            ways = ((0, place.h), (1, 1 - place.h)) if halves else ((None, place.h),)
            for k, (half, h) in enumerate(ways):
                ref = get(sel, half)
                sender.start(ref, ref, sem + k, place.at(z=other, h=h))
            if final:
                mirror(base + 10)
            yield
            for k, (half, h) in enumerate(ways):
                sender.arrived(get({**sel, "z": other}, half), sem + k, place.at(z=other, h=h))
            if final:
                mirror(base + 11, z=other)
            sem += 2
        else:
            a = sel[dim]
            own = get(sel, None)
            for k, step in enumerate((1, -1, 2)):
                sender.start(own, own, sem + k, place.along(dim, step))
            if final:
                mirror(base + 10)
            yield
            for k, step in enumerate((-1, 1, 2)):
                there = lax.rem(a + 4 + step, 4)
                sender.arrived(get({**sel, dim: there}, None), sem + k, place.along(dim, step))
                if final:
                    mirror(base + 11 + k, **{dim: there})
            sem += 3
        sel[dim] = ALL
    yield
    for ref, index in mirrored:
        sender.arrived(ref, index, partner)


def run_streams(streams):
    live = list(streams)
    while live:
        left = []
        for s in live:
            try:
                next(s)
                left.append(s)
            except StopIteration:
                pass
        live = left


def advance(streams):
    for s in streams:
        next(s, None)


REDUCE_ORDERS = (("x", "y", "zz"), ("y", "zz", "x"), ("zz", "x", "y"), ("zz", "y", "x"))


def reduce_part(place, sender, base, p, order, total, wide, narrow, last, out_ref):
    where = {d: None for d in DIMS}

    def cut(dim, index):
        parts = []
        for d in DIMS:
            if d == dim:
                parts.append(index)
            else:
                parts.append(ALL if where[d] is None else where[d])
        return (p, *parts)

    for phase, dim in enumerate(order):
        a = getattr(place, dim)
        slots = (wide, narrow, last)[phase]
        sem = base + 3 * phase
        for k, step in enumerate((1, -1, 2)):
            there = lax.rem(a + 4 + step, 4)
            sender.start(
                total.at[cut(dim, there)], slots.at[p, k], sem + k, place.along(dim, step)
            )
        yield
        for k, step in enumerate((-1, 1, 2)):
            sender.arrived(slots.at[p, k], sem + k, place.along(dim, step))
        i = cut(dim, a)
        value = (total[i] + slots[p, 0]) + (slots[p, 1] + slots[p, 2])
        if phase == 2:
            out_ref[8 * p : 8 * p + 8, :] = value
        else:
            total[i] = value
        where[dim] = a


GROUPS = ((0, 1), (1, 3), (3, 6))


def head_kernel(
    targets_ref, sources_ref, emb_ref, signs_ref, gaussian_ref, scales_ref, phases_ref,
    weights_ref, perms_ref,
    out_ref, line_ref,
    gathered7, places_all, places_ref, perms, emb32, part, first, placed, feats,
    outgoing, theirs, total, wide, narrow, last, lines,
    send, recv, own,
):
    place = Place()
    x, y, z, c, h = place.x, place.y, place.z, place.c, place.h
    partner = place.at(c=1 - c)
    me = ((x * 4 + y) * 2 + z) * 2 + c
    given = [signs_ref, None, gaussian_ref, scales_ref, phases_ref, weights_ref]
    copies = []
    for v, ref in enumerate(given):
        if ref is not None:
            copies.append(pltpu.make_async_copy(ref, gathered7.at[v, x, y, z, c], own.at[v]))
    get_perms = pltpu.make_async_copy(perms_ref, perms, own.at[6])
    for copy in copies:
        copy.start()
    get_perms.start()
    places_all[x, y, z, c, 0:1, 0:64] = sources_ref[...]
    greet(place)
    for copy in copies:
        copy.wait()
    sender = Sender(send, recv)

    def getter(group, quarter):
        vs = slice(*GROUPS[group])

        def get(sel, half):
            rows = pl.ds(16 * quarter, 16) if half is None else pl.ds(16 * quarter + 8 * half, 8)
            return gathered7.at[vs, sel["x"], sel["y"], sel["z"], sel["c"], rows, :]

        return get

    def get_places(sel, half):
        return places_all.at[sel["x"], sel["y"], sel["z"], sel["c"]]

    def get_lines(sel, half):
        return lines.at[sel["x"], sel["y"], sel["z"], sel["c"]]

    groups = []
    for group in range(3):
        groups.append([])
        for q in range(4):
            base = STREAM_SEMS * (4 * group + q)
            groups[group].append(
                gather_stream(place, sender, base, ORDERS[q], getter(group, q), True)
            )
    groups[0].append(gather_stream(place, sender, STREAM_SEMS * 12, "zyx", get_places, False))

    advance(groups[0])
    get_perms.wait()
    lanes = lax.broadcasted_iota(jnp.int32, (8, LANES), 1).astype(F32).astype(BF16)

    def order_of(t, _):
        rows = []
        for q in range(8):
            line = lax.dot_general(
                lanes, perms[8 * t + q], (((1,), (1,)), ((), ())), preferred_element_type=F32
            )
            rows.append(line[0:1])
        gathered7[1, x, y, z, c, pl.ds(pl.multiple_of(8 * t, 8), 8), :] = jnp.concatenate(rows, axis=0)
        return 0

    lax.fori_loop(0, 8, order_of, 0)
    advance(groups[1])
    advance(groups[0])
    advance(groups[2])
    advance(groups[1])
    advance(groups[0])
    advance(groups[2])
    advance(groups[1])
    advance(groups[2])
    gathered = gathered7.reshape(6, N_BLOCKS, LANES)

    h1 = signs_128()
    h2 = jnp.concatenate([h1, h1], axis=0)
    for d in range(4):
        emb32[d] = emb_ref[:, d * LANES : (d + 1) * LANES].astype(F32)
    emb = [[emb32[d, pl.ds(2 * me + r, 1), :] for d in range(4)] for r in range(2)]

    advance(groups[0])
    advance(groups[0])
    to_smem = pltpu.make_async_copy(places_all, places_ref, own.at[7])
    to_smem.start()

    for k_hi in range(8):
        for d in range(4):
            s = gathered[0, pl.ds(512 * k_hi + d, LANES, stride=4), :]
            part[k_hi, d] = jnp.dot(h1, s.astype(BF16), preferred_element_type=F32)

    def stage_u(t, _):
        rows = pl.ds(pl.multiple_of(8 * t, 8), 8)
        cols = []
        for d in range(4):
            cols.append(butterfly([part[k, d, rows, :] for k in range(8)]))
        for k in range(8):
            for r in range(2):
                u = butterfly([emb[r][d] * cols[d][k] for d in range(4)])
                for b in range(4):
                    placed[r, pl.ds(512 * k + 32 * t + b, 8, stride=4), :] = u[b]
        return 0

    lax.fori_loop(0, 16, stage_u, 0)

    for r in range(2):

        def stage_f(t, _, r=r):
            rows = pl.ds(pl.multiple_of(256 * t, 256), 256)
            first[r, rows, :] = times_h(placed[r, rows, :], h2)
            return 0

        lax.fori_loop(0, 16, stage_f, 0)

    advance(groups[1])
    to_smem.wait()

    def stage_g(t, _):
        for q in range(16):
            b = 16 * t + q
            device = t // 4
            s = places_ref[
                device // 16, lax.rem(device // 4, 4), lax.rem(device // 2, 2),
                lax.rem(device, 2), 0, 16 * lax.rem(t, 4) + q,
            ]
            for r in range(2):
                placed[r, pl.ds(b, 1), :] = first[r, pl.ds(s, 1), :]
        return 0

    lax.fori_loop(0, N_BLOCKS // 16, stage_g, 0)
    advance(groups[1])

    def stage_m(t, _):
        xs = [[], []]
        for q in range(16):
            rows = pl.ds(pl.multiple_of(128 * t + 8 * q, 8), 8)
            order = gathered[1, rows, :].astype(jnp.int32)
            g = gathered[2, rows, :]
            for r in range(2):
                xs[r].append(jnp.take_along_axis(placed[r, rows, :], order, axis=1) * g)
        for r in range(2):
            v = times_h(jnp.concatenate(xs[r], axis=0), h2)
            v = butterfly([v[8 * q : 8 * q + 8] for q in range(16)])
            for q in range(16):
                first[r, pl.ds(pl.multiple_of(128 * t + 8 * q, 8), 8), :] = v[q]
        return 0

    lax.fori_loop(0, 32, stage_m, 0)
    advance(groups[2])

    def stage_b(t, _):
        rows = [pl.ds(pl.multiple_of(128 * k + 8 * t, 8), 8) for k in range(32)]
        for r in range(2):
            v = butterfly([first[r, rows[k], :] for k in range(32)])
            for k in range(32):
                first[r, rows[k], :] = v[k]
        return 0

    lax.fori_loop(0, 16, stage_b, 0)
    advance(groups[2])

    def stage_c(t, acc):
        rows = [pl.ds(64 * t + s, 8, stride=8) for s in range(8)]
        ys = [butterfly([first[r, rows[s], :] for s in range(8)]) for r in range(2)]
        acc = list(acc)
        for s in range(8):
            scale = gathered[3, rows[s], :] * (1.0 / FEATURE_COUNT)
            phase = gathered[4, rows[s], :]
            weight = gathered[5, rows[s], :]
            for r in range(2):
                f = cosine(scale * ys[r][s] + phase)
                feats[r, rows[s], :] = f
                acc[r] = acc[r] + f * weight
        return tuple(acc)

    zero = jnp.zeros((8, LANES), F32)
    acc = lax.fori_loop(0, 64, stage_c, (zero, zero))
    line = jnp.zeros((1, LANES), F32)
    lane = lax.broadcasted_iota(jnp.int32, (1, LANES), 1)
    residual = []
    for r in range(2):
        p = jnp.sum(acc[r], axis=(0, 1), keepdims=True) * (1.0 / math.sqrt(FEATURE_COUNT))
        line = jnp.where(lane == 2 * me + r, p, line)
        residual.append((p - targets_ref[2 * me + r]) * (1.0 / 16.0))
    lines[x, y, z, c] = line

    def gradients(p, core, t):
        row = (t // 4) * 256 + lax.rem(t, 2) * 128 + core * 64 + lax.rem(t // 2, 2) * 32 + 8 * p
        rows = pl.ds(pl.multiple_of(row, 8), 8)
        return feats[0, rows, :] * residual[0] + feats[1, rows, :] * residual[1]

    base = STREAM_SEMS * 13
    for p in range(4):

        def stage_o(t, _, p=p):
            for q in range(4):
                i = 4 * t + q
                outgoing[p, t // 4, lax.rem(t, 4), q] = gradients(p, 1 - c, i)
            return 0

        lax.fori_loop(0, 16, stage_o, 0)
        sender.start(outgoing.at[p], theirs.at[p], base + 10 * p, partner)

    def part_stream(p):
        sender.arrived(theirs.at[p], base + 10 * p, partner)

        def stage_s(t, _):
            for q in range(4):
                i = 4 * t + q
                at = (p, t // 4, lax.rem(t, 4), q)
                total[at] = gradients(p, c, i) + theirs[at]
            return 0

        lax.fori_loop(0, 16, stage_s, 0)
        yield from reduce_part(
            place, sender, base + 10 * p + 1, p, REDUCE_ORDERS[p], total, wide, narrow, last, out_ref
        )

    line_stream = gather_stream(place, sender, base + 40, "zyx", get_lines, False)
    run_streams([part_stream(p) for p in range(4)] + [line_stream])
    line = jnp.zeros((1, LANES), F32)
    for i in range(64):
        line = line + lines[i // 16, (i // 4) % 4, (i // 2) % 2, i % 2]
    line_ref[...] = line
    sender.finish()


N_SEMS = STREAM_SEMS * 13 + 40 + STREAM_SEMS


def local(
    embeddings,
    sign_flips,
    gaussian,
    scales,
    phases,
    source_blocks,
    block_permutations,
    weights,
    targets,
):
    rows = lambda v: v.reshape(-1, LANES)
    vmem = pl.BlockSpec(memory_space=pltpu.VMEM)
    smem = pl.BlockSpec(memory_space=pltpu.SMEM)
    any_ = pl.BlockSpec(memory_space=pl.ANY)
    field = pltpu.VMEM((2, N_BLOCKS, LANES), F32)
    tiles = lambda *shape: pltpu.VMEM(shape + (8, LANES), F32)
    grad_out, line = pl.pallas_call(
        head_kernel,
        out_shape=(
            jax.ShapeDtypeStruct((32, LANES), F32),
            jax.ShapeDtypeStruct((1, LANES), F32),
        ),
        in_specs=[smem, vmem, vmem] + [any_] * 6,
        out_specs=(vmem, vmem),
        scratch_shapes=[
            pltpu.VMEM((6, 4, 4, 2, 2, 64, LANES), F32),
            pltpu.VMEM((4, 4, 2, 2, 1, LANES), jnp.int32),
            pltpu.SMEM((4, 4, 2, 2, 1, LANES), jnp.int32),
            pltpu.VMEM((64, LANES, LANES), BF16),
            pltpu.VMEM((4, 128, LANES), F32),
            pltpu.VMEM((8, 4, LANES, LANES), F32),
            field, field, field,
            tiles(4, 4, 4, 4), tiles(4, 4, 4, 4), tiles(4, 4, 4, 4),
            tiles(4, 3, 4, 4), tiles(4, 3, 4), tiles(4, 3),
            pltpu.VMEM((4, 4, 2, 2, 1, LANES), F32),
            pltpu.SemaphoreType.DMA((N_SEMS,)),
            pltpu.SemaphoreType.DMA((N_SEMS,)),
            pltpu.SemaphoreType.DMA((8,)),
        ],
        compiler_params=pltpu.CompilerParams(
            vmem_limit_bytes=60 * 2**20, collective_id=0, has_side_effects=True
        ),
    )(
        targets, source_blocks.reshape(1, -1), embeddings, rows(sign_flips), rows(gaussian),
        rows(scales), rows(phases), rows(weights), block_permutations,
    )
    return line.reshape(-1), grad_out.reshape(-1)


def solution(mesh):
    in_specs = (
        P("rows", None), P("feat"), P("feat"), P("feat"), P("feat"), P("feat"),
        P("feat", None, None), P("feat"), P("rows"),
    )
    out_specs = (P("rows"), P(("feat", "rows")))
    return jax.shard_map(local, mesh=mesh, in_specs=in_specs, out_specs=out_specs, check_vma=False)
```

```python
import functools
import math

import jax
import jax.numpy as jnp
from jax import lax
from jax.experimental import pallas as pl
from jax.experimental.pallas import tpu as pltpu
from jax.sharding import PartitionSpec as P

FEATURE_COUNT = 524288
LANES = 128
N_BLOCKS = 4096
F32 = jnp.float32
BF16 = jnp.bfloat16


def signs_128():
    i = lax.broadcasted_iota(jnp.int32, (LANES, LANES), 0)
    j = lax.broadcasted_iota(jnp.int32, (LANES, LANES), 1)
    v = jnp.bitwise_and(i, j)
    v = jnp.bitwise_xor(v, jnp.right_shift(v, 4))
    v = jnp.bitwise_xor(v, jnp.right_shift(v, 2))
    v = jnp.bitwise_xor(v, jnp.right_shift(v, 1))
    return (1 - 2 * jnp.bitwise_and(v, 1)).astype(F32).astype(BF16)


def times_h(x, h2):
    a = x.astype(BF16)
    b = (x - a.astype(F32)).astype(BF16)
    return jnp.dot(jnp.concatenate([a, b], axis=1), h2, preferred_element_type=F32)


def butterfly(values):
    n = len(values)
    half = 1
    values = list(values)
    while half < n:
        out = [None] * n
        for base in range(0, n, 2 * half):
            for k in range(half):
                u, v = values[base + k], values[base + half + k]
                out[base + k] = u + v
                out[base + half + k] = u - v
        values = out
        half *= 2
    return values


TWO_PI_A = 6.28125
TWO_PI_B = 2.0 * math.pi - 6.28125


def cos_coefficients():
    import numpy as np

    n = 7
    k = np.arange(n)
    u = 0.5 * math.pi**2 * (1.0 + np.cos((k + 0.5) * math.pi / n)) * 1.01
    v = np.stack([u**p for p in range(n)], axis=1)
    c = np.linalg.solve(v, np.cos(np.sqrt(u)))
    return [float(x) for x in c]


COS = cos_coefficients()


def cosine(x):
    n = jnp.round(x * (1.0 / (2.0 * math.pi)))
    r = (x - n * TWO_PI_A) - n * TWO_PI_B
    u = r * r
    acc = COS[-1] * u + COS[-2]
    for c in COS[-3::-1]:
        acc = acc * u + c
    return acc


MESH = pl.DeviceIdType.MESH
ALL = slice(None)
ORDERS = ("yzx", "xzy", "xyz", "yxz")
STREAM_SEMS = 14
DIMS = ("x", "y", "zz")


class Place:
    def __init__(self):
        me = lax.axis_index("feat")
        self.h = lax.axis_index("rows")
        self.c = lax.rem(me, 2)
        self.z = lax.rem(me // 2, 2)
        self.y = lax.rem(me // 4, 4)
        self.x = me // 16
        self.zz = 2 * self.h + self.z

    def at(self, x=None, y=None, z=None, c=None, h=None):
        x = self.x if x is None else x
        y = self.y if y is None else y
        z = self.z if z is None else z
        c = self.c if c is None else c
        h = self.h if h is None else h
        return (((x * 4 + y) * 2 + z) * 2 + c, h)

    def along(self, dim, step):
        a = lax.rem(getattr(self, dim) + 4 + step, 4)
        if dim == "zz":
            return self.at(z=lax.rem(a, 2), h=a // 2)
        return self.at(**{dim: a})

    def neighbours(self):
        out = [self.along(d, s) for d in DIMS for s in (1, -1, 2)]
        return out + [self.at(c=1 - self.c)]


def greet(place):
    barrier = pltpu.get_barrier_semaphore()
    others = place.neighbours()
    for device in others:
        pl.semaphore_signal(barrier, inc=1, device_id=device, device_id_type=MESH)
    pl.semaphore_wait(barrier, len(others))


PLAN = (
    0, 2, 3, 4, "order", 1,
    0, 1, 0, 2, 3, 4, 1, 2, 3, 4,
    0, 0, "t", "f", ("g", 0, 64),
    1, 1, ("m", 0, 16),
    2, ("m", 16, 32),
    3, ("b", 0, 16),
    4, 2, 3, ("c", 0, 64), 4,
)


class Sender:
    def __init__(self, send, recv):
        self.send, self.recv = send, recv
        self.started = []

    def copy(self, ref, dst, sem, device):
        return pltpu.make_async_remote_copy(
            src_ref=ref, dst_ref=dst, send_sem=self.send.at[sem], recv_sem=self.recv.at[sem],
            device_id=device, device_id_type=MESH,
        )

    def start(self, ref, dst, sem, device):
        copy = self.copy(ref, dst, sem, device)
        copy.start()
        self.started.append(copy)

    def arrived(self, ref, sem, device):
        self.copy(ref, ref, sem, device).wait_recv()

    def finish(self):
        for copy in self.started:
            copy.wait_send()


def gather_stream(place, sender, base, order, get, halves):
    sel = {"x": place.x, "y": place.y, "z": place.z, "c": place.c}
    partner = place.at(c=1 - place.c)
    sem = base
    mirrored = []

    def mirror(index, **where):
        here = get({**sel, **where}, None)
        sender.start(here, here, index, partner)
        mirrored.append((get({**sel, **where, "c": 1 - place.c}, None), index))

    for phase, dim in enumerate(order):
        final = phase == 2
        if dim == "z":
            other = 1 - place.z
            ways = ((0, place.h), (1, 1 - place.h)) if halves else ((None, place.h),)
            for k, (half, h) in enumerate(ways):
                ref = get(sel, half)
                sender.start(ref, ref, sem + k, place.at(z=other, h=h))
            if final:
                mirror(base + 10)
            yield
            for k, (half, h) in enumerate(ways):
                sender.arrived(get({**sel, "z": other}, half), sem + k, place.at(z=other, h=h))
            if final:
                mirror(base + 11, z=other)
            sem += 2
        else:
            a = sel[dim]
            own = get(sel, None)
            for k, step in enumerate((1, -1, 2)):
                sender.start(own, own, sem + k, place.along(dim, step))
            if final:
                mirror(base + 10)
            yield
            for k, step in enumerate((-1, 1, 2)):
                there = lax.rem(a + 4 + step, 4)
                sender.arrived(get({**sel, dim: there}, None), sem + k, place.along(dim, step))
                if final:
                    mirror(base + 11 + k, **{dim: there})
            sem += 3
        sel[dim] = ALL
    yield
    for ref, index in mirrored:
        sender.arrived(ref, index, partner)


def run_streams(streams):
    live = list(streams)
    while live:
        left = []
        for s in live:
            try:
                next(s)
                left.append(s)
            except StopIteration:
                pass
        live = left


def advance(streams):
    for s in streams:
        next(s, None)


class Reducer:
    def __init__(self, place, sender, total):
        self.place, self.sender, self.total = place, sender, total

    def entry(self, p, sel, dim, a):
        here = {**sel, "z": lax.rem(a, 2), "h": a // 2} if dim == "zz" else {**sel, dim: a}
        return (p, *(here[d] for d in "xyzh"))

    def start(self, p, sel, dim, slots, sem):
        a = getattr(self.place, dim)
        for k, step in enumerate((1, -1, 2)):
            there = lax.rem(a + 4 + step, 4)
            self.sender.start(
                self.total.at[self.entry(p, sel, dim, there)], slots.at[k], sem + k,
                self.place.along(dim, step),
            )

    def finish(self, p, sel, dim, slots, sem):
        for k, step in enumerate((-1, 1, 2)):
            self.sender.arrived(slots.at[k], sem + k, self.place.along(dim, step))
        i = self.entry(p, sel, dim, getattr(self.place, dim))
        value = (self.total[i] + slots[0]) + (slots[1] + slots[2])
        self.total[i] = value
        return i, value

    def pinned(self, dim):
        if dim == "zz":
            return {"z": self.place.z, "h": self.place.h}
        return {dim: getattr(self.place, dim)}

    def rings(self, p, sel, order, slots, sem):
        for dim, slot in zip(order, slots):
            self.start(p, sel, dim, slot, sem)
            yield
            value = self.finish(p, sel, dim, slot, sem)[1]
            sel = {**sel, **self.pinned(dim)}
            sem += 3
        return value


def reduce_scratch():
    shapes = [(4, 2, 2), (2, 2), (), (4, 2, 2), (4,), (), (4, 4), (4,), ()]
    shapes += [(4, 2), (2,), (4, 2), (2,), ()]
    return [pltpu.VMEM((3,) + shape + (8, LANES), F32) for shape in shapes]


GROUPS = ((0, 1), (1, 3), (3, 4), (4, 5), (5, 6))


def head_kernel(
    targets_ref, sources_ref, emb_ref, signs_ref, gaussian_ref, scales_ref, phases_ref,
    weights_ref, perms_ref,
    out_ref, line_ref,
    gathered7, places_all, places_ref, perms, emb32, part, first, placed, feats,
    outgoing, theirs, total, lines,
    send, recv, own, *slots,
):
    place = Place()
    x, y, z, c, h = place.x, place.y, place.z, place.c, place.h
    partner = place.at(c=1 - c)
    me = ((x * 4 + y) * 2 + z) * 2 + c
    given = [signs_ref, None, gaussian_ref, scales_ref, phases_ref, weights_ref]
    copies = []
    for v, ref in enumerate(given):
        if ref is not None:
            copies.append(pltpu.make_async_copy(ref, gathered7.at[v, x, y, z, c], own.at[v]))
    get_perms = pltpu.make_async_copy(perms_ref, perms, own.at[6])
    for copy in copies:
        copy.start()
    get_perms.start()
    places_all[x, y, z, c, 0:1, 0:64] = sources_ref[...]
    greet(place)
    for copy in copies:
        copy.wait()
    sender = Sender(send, recv)

    def getter(group, quarter):
        vs = slice(*GROUPS[group])

        def get(sel, half):
            rows = pl.ds(16 * quarter, 16) if half is None else pl.ds(16 * quarter + 8 * half, 8)
            return gathered7.at[vs, sel["x"], sel["y"], sel["z"], sel["c"], rows, :]

        return get

    def get_places(sel, half):
        return places_all.at[sel["x"], sel["y"], sel["z"], sel["c"]]

    def get_lines(sel, half):
        return lines.at[sel["x"], sel["y"], sel["z"], sel["c"]]

    groups = []
    for group in range(len(GROUPS)):
        groups.append([])
        for q in range(4):
            base = STREAM_SEMS * (4 * group + q)
            groups[group].append(
                gather_stream(place, sender, base, ORDERS[q], getter(group, q), True)
            )
    groups[0].append(gather_stream(place, sender, STREAM_SEMS * 4 * len(GROUPS), "zyx", get_places, False))

    lanes = lax.broadcasted_iota(jnp.int32, (8, LANES), 1).astype(F32).astype(BF16)

    gathered = gathered7.reshape(6, N_BLOCKS, LANES)

    h1 = signs_128()
    h2 = jnp.concatenate([h1, h1], axis=0)
    for d in range(4):
        emb32[d] = emb_ref[:, d * LANES : (d + 1) * LANES].astype(F32)
    emb = [[emb32[d, pl.ds(2 * me + r, 1), :] for d in range(4)] for r in range(2)]

    def order_of(t, _):
        rows = []
        for q in range(8):
            line = lax.dot_general(
                lanes, perms[8 * t + q], (((1,), (1,)), ((), ())), preferred_element_type=F32
            )
            rows.append(line[0:1])
        gathered7[1, x, y, z, c, pl.ds(pl.multiple_of(8 * t, 8), 8), :] = jnp.concatenate(rows, axis=0)
        return 0

    def stage_t():
        for k_hi in range(8):
            for d in range(4):
                s = gathered[0, pl.ds(512 * k_hi + d, LANES, stride=4), :]
                part[k_hi, d] = jnp.dot(h1, s.astype(BF16), preferred_element_type=F32)

    def stage_u(t, _):
        rows = pl.ds(pl.multiple_of(8 * t, 8), 8)
        cols = []
        for d in range(4):
            cols.append(butterfly([part[k, d, rows, :] for k in range(8)]))
        for k in range(8):
            for r in range(2):
                u = butterfly([emb[r][d] * cols[d][k] for d in range(4)])
                for b in range(4):
                    placed[r, pl.ds(512 * k + 32 * t + b, 8, stride=4), :] = u[b]
        return 0

    def stage_f(t, _):
        rows = pl.ds(pl.multiple_of(256 * t, 256), 256)
        for r in range(2):
            first[r, rows, :] = times_h(placed[r, rows, :], h2)
        return 0

    def stage_g(t, _):
        for q in range(64):
            s = places_ref[t, 0, q]
            for r in range(2):
                placed[r, pl.ds(64 * t + q, 1), :] = first[r, pl.ds(s, 1), :]
        return 0

    def stage_m(t, _):
        xs = [[], []]
        for q in range(16):
            rows = pl.ds(pl.multiple_of(128 * t + 8 * q, 8), 8)
            order = gathered[1, rows, :].astype(jnp.int32)
            g = gathered[2, rows, :]
            for r in range(2):
                xs[r].append(jnp.take_along_axis(placed[r, rows, :], order, axis=1) * g)
        for r in range(2):
            v = times_h(jnp.concatenate(xs[r], axis=0), h2)
            v = butterfly([v[8 * q : 8 * q + 8] for q in range(16)])
            for q in range(16):
                first[r, pl.ds(pl.multiple_of(128 * t + 8 * q, 8), 8), :] = v[q]
        return 0

    def stage_b(t, _):
        rows = [pl.ds(pl.multiple_of(128 * k + 8 * t, 8), 8) for k in range(32)]
        for r in range(2):
            v = butterfly([first[r, rows[k], :] for k in range(32)])
            for k in range(32):
                first[r, rows[k], :] = v[k]
        return 0

    def stage_c(t, _):
        rows = [pl.ds(64 * t + s, 8, stride=8) for s in range(8)]
        ys = [butterfly([first[r, rows[s], :] for s in range(8)]) for r in range(2)]
        for s in range(8):
            scale = gathered[3, rows[s], :] * (1.0 / FEATURE_COUNT)
            phase = gathered[4, rows[s], :]
            for r in range(2):
                feats[r, rows[s], :] = cosine(scale * ys[r][s] + phase)
        return 0

    def stage_d(t, acc):
        out = []
        rows = [pl.ds(pl.multiple_of(128 * t + 8 * q, 8), 8) for q in range(16)]
        weight = [gathered[5, rows[q], :] for q in range(16)]
        for r in range(2):
            v = [feats[r, rows[q], :] * weight[q] for q in range(16)]
            while len(v) > 1:
                v = [v[k] + v[k + 1] for k in range(0, len(v), 2)]
            out.append(acc[r] + v[0])
        return tuple(out)

    to_smem = pltpu.make_async_copy(places_all.reshape(64, 1, LANES), places_ref, own.at[7])
    for step in PLAN:
        if isinstance(step, int):
            advance(groups[step])
        elif step == "order":
            get_perms.wait()
            lax.fori_loop(0, 8, order_of, 0)
        elif step == "t":
            to_smem.start()
            stage_t()
            lax.fori_loop(0, 16, stage_u, 0, unroll=2)
        elif step == "f":
            lax.fori_loop(0, 16, stage_f, 0, unroll=8)
            to_smem.wait()
        else:
            stage, low, high = step
            loop, unroll = {
                "g": (stage_g, 1), "m": (stage_m, 4), "b": (stage_b, 1), "c": (stage_c, 4)
            }[stage]
            lax.fori_loop(low, high, loop, 0, unroll=unroll)

    zero = jnp.zeros((8, LANES), F32)
    acc = lax.fori_loop(0, 32, stage_d, (zero, zero))
    line = jnp.zeros((1, LANES), F32)
    lane = lax.broadcasted_iota(jnp.int32, (1, LANES), 1)
    residual = []
    for r in range(2):
        p = jnp.sum(acc[r], axis=(0, 1), keepdims=True) * (1.0 / math.sqrt(FEATURE_COUNT))
        line = jnp.where(lane == 2 * me + r, p, line)
        residual.append((p - targets_ref[2 * me + r]) * (1.0 / 16.0))
    lines[x, y, z, c] = line

    def gradients(p, core, t):
        out = []
        for i in range(16):
            row = 1024 * t + (i // 4) * 256 + ((i // 2) % 2) * 128 + (i % 2) * 32 + 8 * p + core * 64
            rows = pl.ds(pl.multiple_of(row, 8), 8)
            out.append(feats[0, rows, :] * residual[0] + feats[1, rows, :] * residual[1])
        return out

    for p in range(4):

        def stage_o(t, _, p=p):
            for i, value in enumerate(gradients(p, 1 - c, t)):
                outgoing[p, t, i // 4, (i // 2) % 2, i % 2] = value
            return 0

        lax.fori_loop(0, 4, stage_o, 0, unroll=2)
        sender.start(outgoing.at[p], theirs.at[p], REDUCE_BASE + p, partner)

    reducer = Reducer(place, sender, total)
    whole = {d: ALL for d in "xyzh"}

    def add_theirs(p):
        sender.arrived(theirs.at[p], REDUCE_BASE + p, partner)

        def stage_s(t, _):
            values = gradients(p, c, t)
            values = [v + theirs[p, t, i // 4, (i // 2) % 2, i % 2] for i, v in enumerate(values)]
            for i, value in enumerate(values):
                total[p, t, i // 4, (i // 2) % 2, i % 2] = value
            return 0

        lax.fori_loop(0, 4, stage_s, 0, unroll=2)

    def part_stream(p, order, sem):
        add_theirs(p)
        value = yield from reducer.rings(p, whole, order, slots[3 * p : 3 * p + 3], sem)
        out_ref[8 * p : 8 * p + 8, :] = value

    def last_stream(sem):
        add_theirs(3)
        halves = [
            reducer.rings(3, {**whole, "z": k}, order, slots[9 + 2 * k : 11 + 2 * k], sem + 6 * k)
            for k, order in enumerate((("x", "y"), ("y", "x")))
        ]
        for _ in range(3):
            advance(halves)
            if _ < 2:
                yield
        sel = {**whole, "x": x, "y": y}
        value = yield from reducer.rings(3, sel, ("zz",), slots[13:14], sem + 12)
        out_ref[24:32, :] = value

    sem = REDUCE_BASE + 4
    run_streams(
        [
            part_stream(0, ("x", "y", "zz"), sem),
            part_stream(1, ("y", "zz", "x"), sem + 9),
            part_stream(2, ("zz", "x", "y"), sem + 18),
            last_stream(sem + 27),
            gather_stream(place, sender, REDUCE_BASE + 50, "zyx", get_lines, False),
        ]
    )
    line = jnp.zeros((1, LANES), F32)
    for i in range(64):
        line = line + lines[i // 16, (i // 4) % 4, (i // 2) % 2, i % 2]
    line_ref[...] = line
    sender.finish()


REDUCE_BASE = STREAM_SEMS * (4 * len(GROUPS) + 1)
N_SEMS = REDUCE_BASE + 50 + STREAM_SEMS


def local(
    embeddings,
    sign_flips,
    gaussian,
    scales,
    phases,
    source_blocks,
    block_permutations,
    weights,
    targets,
):
    rows = lambda v: v.reshape(-1, LANES)
    vmem = pl.BlockSpec(memory_space=pltpu.VMEM)
    smem = pl.BlockSpec(memory_space=pltpu.SMEM)
    any_ = pl.BlockSpec(memory_space=pl.ANY)
    field = pltpu.VMEM((2, N_BLOCKS, LANES), F32)
    tiles = lambda *shape: pltpu.VMEM(shape + (8, LANES), F32)
    grad_out, line = pl.pallas_call(
        head_kernel,
        out_shape=(
            jax.ShapeDtypeStruct((32, LANES), F32),
            jax.ShapeDtypeStruct((1, LANES), F32),
        ),
        in_specs=[smem, vmem, vmem] + [any_] * 6,
        out_specs=(vmem, vmem),
        scratch_shapes=[
            pltpu.VMEM((6, 4, 4, 2, 2, 64, LANES), F32),
            pltpu.VMEM((4, 4, 2, 2, 1, LANES), jnp.int32),
            pltpu.SMEM((64, 1, LANES), jnp.int32),
            pltpu.VMEM((64, LANES, LANES), BF16),
            pltpu.VMEM((4, 128, LANES), F32),
            pltpu.VMEM((8, 4, LANES, LANES), F32),
            field, field, field,
            tiles(4, 4, 4, 2, 2), tiles(4, 4, 4, 2, 2), tiles(4, 4, 4, 2, 2),
            pltpu.VMEM((4, 4, 2, 2, 1, LANES), F32),
            pltpu.SemaphoreType.DMA((N_SEMS,)),
            pltpu.SemaphoreType.DMA((N_SEMS,)),
            pltpu.SemaphoreType.DMA((8,)),
            *reduce_scratch(),
        ],
        compiler_params=pltpu.CompilerParams(
            vmem_limit_bytes=60 * 2**20, collective_id=0, has_side_effects=True
        ),
    )(
        targets, source_blocks.reshape(1, -1), embeddings, rows(sign_flips), rows(gaussian),
        rows(scales), rows(phases), rows(weights), block_permutations,
    )
    return line.reshape(-1), grad_out.reshape(-1)


def solution(mesh):
    in_specs = (
        P("rows", None), P("feat"), P("feat"), P("feat"), P("feat"), P("feat"),
        P("feat", None, None), P("feat"), P("rows"),
    )
    out_specs = (P("rows"), P(("feat", "rows")))
    return jax.shard_map(local, mesh=mesh, in_specs=in_specs, out_specs=out_specs, check_vma=False)
```

```python
import functools
import math

import jax
import jax.numpy as jnp
from jax import lax
from jax.experimental import pallas as pl
from jax.experimental.pallas import tpu as pltpu
from jax.sharding import PartitionSpec as P

FEATURE_COUNT = 524288
LANES = 128
N_BLOCKS = 4096
F32 = jnp.float32
BF16 = jnp.bfloat16


def signs_128():
    i = lax.broadcasted_iota(jnp.int32, (LANES, LANES), 0)
    j = lax.broadcasted_iota(jnp.int32, (LANES, LANES), 1)
    v = jnp.bitwise_and(i, j)
    v = jnp.bitwise_xor(v, jnp.right_shift(v, 4))
    v = jnp.bitwise_xor(v, jnp.right_shift(v, 2))
    v = jnp.bitwise_xor(v, jnp.right_shift(v, 1))
    return (1 - 2 * jnp.bitwise_and(v, 1)).astype(F32).astype(BF16)


def times_h(x, h2):
    a = x.astype(BF16)
    b = (x - a.astype(F32)).astype(BF16)
    return jnp.dot(jnp.concatenate([a, b], axis=1), h2, preferred_element_type=F32)


def butterfly(values):
    n = len(values)
    half = 1
    values = list(values)
    while half < n:
        out = [None] * n
        for base in range(0, n, 2 * half):
            for k in range(half):
                u, v = values[base + k], values[base + half + k]
                out[base + k] = u + v
                out[base + half + k] = u - v
        values = out
        half *= 2
    return values


TWO_PI_A = 6.28125
TWO_PI_B = 2.0 * math.pi - 6.28125


def cos_coefficients():
    import numpy as np

    n = 7
    k = np.arange(n)
    u = 0.5 * math.pi**2 * (1.0 + np.cos((k + 0.5) * math.pi / n)) * 1.01
    v = np.stack([u**p for p in range(n)], axis=1)
    c = np.linalg.solve(v, np.cos(np.sqrt(u)))
    return [float(x) for x in c]


COS = cos_coefficients()


def cosine(x):
    n = jnp.round(x * (1.0 / (2.0 * math.pi)))
    r = (x - n * TWO_PI_A) - n * TWO_PI_B
    u = r * r
    acc = COS[-1] * u + COS[-2]
    for c in COS[-3::-1]:
        acc = acc * u + c
    return acc


MESH = pl.DeviceIdType.MESH
ALL = slice(None)
ORDERS = ("yzx", "xzy", "xyz", "yxz")
RELAYED = (2,)
STREAM_SEMS = 14
DIMS = ("x", "y", "zz")


class Place:
    def __init__(self):
        me = lax.axis_index("feat")
        self.h = lax.axis_index("rows")
        self.c = lax.rem(me, 2)
        self.z = lax.rem(me // 2, 2)
        self.y = lax.rem(me // 4, 4)
        self.x = me // 16
        self.zz = 2 * self.h + self.z

    def at(self, x=None, y=None, z=None, c=None, h=None):
        x = self.x if x is None else x
        y = self.y if y is None else y
        z = self.z if z is None else z
        c = self.c if c is None else c
        h = self.h if h is None else h
        return (((x * 4 + y) * 2 + z) * 2 + c, h)

    def along(self, dim, step):
        a = lax.rem(getattr(self, dim) + 4 + step, 4)
        if dim == "zz":
            return self.at(z=lax.rem(a, 2), h=a // 2)
        return self.at(**{dim: a})

    def neighbours(self):
        out = [self.along(d, s) for d in DIMS for s in (1, -1, 2)]
        return out + [self.at(c=1 - self.c)]


def greet(place):
    barrier = pltpu.get_barrier_semaphore()
    others = place.neighbours()
    for device in others:
        pl.semaphore_signal(barrier, inc=1, device_id=device, device_id_type=MESH)
    pl.semaphore_wait(barrier, len(others))


PLAN = (
    0, 2, 3, "order", 1,
    0, 1, 0, 2, 3, 0, 1, 0, 0, "t",
    1, 2, 3, "f", ("g", 0, 32),
    1, ("g", 32, 64),
    2, 1, ("m", 0, 16),
    3, 2, ("m", 16, 32),
    ("b", 0, 16),
    2, 3, ("c", 0, 64), 3,
)


class Sender:
    def __init__(self, send, recv):
        self.send, self.recv = send, recv
        self.started = []

    def copy(self, ref, dst, sem, device):
        return pltpu.make_async_remote_copy(
            src_ref=ref, dst_ref=dst, send_sem=self.send.at[sem], recv_sem=self.recv.at[sem],
            device_id=device, device_id_type=MESH,
        )

    def start(self, ref, dst, sem, device):
        copy = self.copy(ref, dst, sem, device)
        copy.start()
        self.started.append(copy)

    def arrived(self, ref, sem, device):
        self.copy(ref, ref, sem, device).wait_recv()

    def finish(self):
        for copy in self.started:
            copy.wait_send()


def gather_stream(place, sender, base, order, get, halves):
    sel = {"x": place.x, "y": place.y, "z": place.z, "c": place.c}
    partner = place.at(c=1 - place.c)
    sem = base
    mirrored = []

    def mirror(index, **where):
        here = get({**sel, **where}, None)
        sender.start(here, here, index, partner)
        mirrored.append((get({**sel, **where, "c": 1 - place.c}, None), index))

    relays = 0
    for phase, dim in enumerate(order):
        final = phase == 2
        if dim == "z":
            other = 1 - place.z
            ways = ((0, place.h), (1, 1 - place.h)) if halves else ((None, place.h),)
            for k, (half, h) in enumerate(ways):
                ref = get(sel, half)
                sender.start(ref, ref, sem + k, place.at(z=other, h=h))
            if final:
                mirror(base + 10)
            yield
            for k, (half, h) in enumerate(ways):
                sender.arrived(get({**sel, "z": other}, half), sem + k, place.at(z=other, h=h))
            if final:
                mirror(base + 11, z=other)
            sem += 2
        elif halves and phase in RELAYED:
            relays += 1
            a = sel[dim]
            up, down = place.along(dim, 1), place.along(dim, -1)
            below, above, across = (lax.rem(a + k, 4) for k in (3, 1, 2))
            own = get(sel, None)
            sender.start(own, own, sem, up)
            sender.start(own, own, sem + 1, down)
            if final:
                mirror(base + 10)
            yield
            sender.arrived(get({**sel, dim: below}, None), sem, down)
            ref = get({**sel, dim: below}, 0)
            sender.start(ref, ref, sem + 2, up)
            sender.arrived(get({**sel, dim: above}, None), sem + 1, up)
            ref = get({**sel, dim: above}, 1)
            sender.start(ref, ref, sem + 3, down)
            if final:
                mirror(base + 11, **{dim: below})
                mirror(base + 12, **{dim: above})
            yield
            sender.arrived(get({**sel, dim: across}, 0), sem + 2, down)
            sender.arrived(get({**sel, dim: across}, 1), sem + 3, up)
            if final:
                mirror(base + 13, **{dim: across})
            sem += 4
        else:
            a = sel[dim]
            own = get(sel, None)
            for k, step in enumerate((1, -1, 2)):
                sender.start(own, own, sem + k, place.along(dim, step))
            if final:
                mirror(base + 10)
            yield
            for k, step in enumerate((-1, 1, 2)):
                there = lax.rem(a + 4 + step, 4)
                sender.arrived(get({**sel, dim: there}, None), sem + k, place.along(dim, step))
                if final:
                    mirror(base + 11 + k, **{dim: there})
            sem += 3
        sel[dim] = ALL
    yield
    if relays == 0 and RELAYED:
        yield
    for ref, index in mirrored:
        sender.arrived(ref, index, partner)


def run_streams(streams):
    live = list(streams)
    while live:
        left = []
        for s in live:
            try:
                next(s)
                left.append(s)
            except StopIteration:
                pass
        live = left


def advance(streams):
    for s in streams:
        next(s, None)


class Reducer:
    def __init__(self, place, sender, total):
        self.place, self.sender, self.total = place, sender, total

    def entry(self, p, sel, dim, a):
        here = {**sel, "z": lax.rem(a, 2), "h": a // 2} if dim == "zz" else {**sel, dim: a}
        return (p, *(here[d] for d in "xyzh"))

    def start(self, p, sel, dim, slots, sem):
        a = getattr(self.place, dim)
        for k, step in enumerate((1, -1, 2)):
            there = lax.rem(a + 4 + step, 4)
            self.sender.start(
                self.total.at[self.entry(p, sel, dim, there)], slots.at[k], sem + k,
                self.place.along(dim, step),
            )

    def finish(self, p, sel, dim, slots, sem):
        for k, step in enumerate((-1, 1, 2)):
            self.sender.arrived(slots.at[k], sem + k, self.place.along(dim, step))
        i = self.entry(p, sel, dim, getattr(self.place, dim))
        value = (self.total[i] + slots[0]) + (slots[1] + slots[2])
        self.total[i] = value
        return i, value

    def pinned(self, dim):
        if dim == "zz":
            return {"z": self.place.z, "h": self.place.h}
        return {dim: getattr(self.place, dim)}

    def rings(self, p, sel, order, slots, sem):
        for dim, slot in zip(order, slots):
            self.start(p, sel, dim, slot, sem)
            yield
            value = self.finish(p, sel, dim, slot, sem)[1]
            sel = {**sel, **self.pinned(dim)}
            sem += 3
        return value


def reduce_scratch():
    shapes = [(4, 2, 2), (2, 2), (), (4, 2, 2), (4,), (), (4, 4), (4,), ()]
    shapes += [(4, 2), (2,), (4, 2), (2,), ()]
    return [pltpu.VMEM((3,) + shape + (8, LANES), F32) for shape in shapes]


GROUPS = ((0, 1), (1, 3), (3, 5), (5, 6))


def head_kernel(
    targets_ref, sources_ref, emb_ref, signs_ref, gaussian_ref, scales_ref, phases_ref,
    weights_ref, perms_ref,
    out_ref, line_ref,
    gathered7, places_all, places_ref, perms, emb32, part, first, placed, feats,
    outgoing, theirs, total, lines,
    send, recv, own, *slots,
):
    place = Place()
    x, y, z, c, h = place.x, place.y, place.z, place.c, place.h
    partner = place.at(c=1 - c)
    me = ((x * 4 + y) * 2 + z) * 2 + c
    given = [signs_ref, None, gaussian_ref, scales_ref, phases_ref, weights_ref]
    copies = []
    for v, ref in enumerate(given):
        if ref is not None:
            copies.append(pltpu.make_async_copy(ref, gathered7.at[v, x, y, z, c], own.at[v]))
    get_perms = pltpu.make_async_copy(perms_ref, perms, own.at[6])
    for copy in copies:
        copy.start()
    get_perms.start()
    places_all[x, y, z, c, 0:1, 0:64] = sources_ref[...]
    greet(place)
    for copy in copies:
        copy.wait()
    sender = Sender(send, recv)

    def getter(group, quarter):
        vs = slice(*GROUPS[group])

        def get(sel, half):
            rows = pl.ds(16 * quarter, 16) if half is None else pl.ds(16 * quarter + 8 * half, 8)
            return gathered7.at[vs, sel["x"], sel["y"], sel["z"], sel["c"], rows, :]

        return get

    def get_places(sel, half):
        return places_all.at[sel["x"], sel["y"], sel["z"], sel["c"]]

    def get_lines(sel, half):
        return lines.at[sel["x"], sel["y"], sel["z"], sel["c"]]

    groups = []
    for group in range(len(GROUPS)):
        groups.append([])
        for q in range(4):
            base = STREAM_SEMS * (4 * group + q)
            groups[group].append(
                gather_stream(place, sender, base, ORDERS[q], getter(group, q), True)
            )
    groups[0].append(gather_stream(place, sender, STREAM_SEMS * 4 * len(GROUPS), "zyx", get_places, False))

    lanes = lax.broadcasted_iota(jnp.int32, (8, LANES), 1).astype(F32).astype(BF16)

    gathered = gathered7.reshape(6, N_BLOCKS, LANES)

    h1 = signs_128()
    h2 = jnp.concatenate([h1, h1], axis=0)
    for d in range(4):
        emb32[d] = emb_ref[:, d * LANES : (d + 1) * LANES].astype(F32)
    emb = [[emb32[d, pl.ds(2 * me + r, 1), :] for d in range(4)] for r in range(2)]

    def order_of(t, _):
        rows = []
        for q in range(8):
            line = lax.dot_general(
                lanes, perms[8 * t + q], (((1,), (1,)), ((), ())), preferred_element_type=F32
            )
            rows.append(line[0:1])
        gathered7[1, x, y, z, c, pl.ds(pl.multiple_of(8 * t, 8), 8), :] = jnp.concatenate(rows, axis=0)
        return 0

    def stage_t():
        for k_hi in range(8):
            for d in range(4):
                s = gathered[0, pl.ds(512 * k_hi + d, LANES, stride=4), :]
                part[k_hi, d] = jnp.dot(h1, s.astype(BF16), preferred_element_type=F32)

    def stage_u(t, _):
        rows = pl.ds(pl.multiple_of(8 * t, 8), 8)
        cols = []
        for d in range(4):
            cols.append(butterfly([part[k, d, rows, :] for k in range(8)]))
        for k in range(8):
            for r in range(2):
                u = butterfly([emb[r][d] * cols[d][k] for d in range(4)])
                for b in range(4):
                    placed[r, pl.ds(512 * k + 32 * t + b, 8, stride=4), :] = u[b]
        return 0

    def stage_f(t, _):
        rows = pl.ds(pl.multiple_of(256 * t, 256), 256)
        for r in range(2):
            first[r, rows, :] = times_h(placed[r, rows, :], h2)
        return 0

    def stage_g(t, _):
        for q in range(64):
            s = places_ref[t, 0, q]
            for r in range(2):
                placed[r, pl.ds(64 * t + q, 1), :] = first[r, pl.ds(s, 1), :]
        return 0

    def stage_m(t, _):
        xs = [[], []]
        for q in range(16):
            rows = pl.ds(pl.multiple_of(128 * t + 8 * q, 8), 8)
            order = gathered[1, rows, :].astype(jnp.int32)
            g = gathered[2, rows, :]
            for r in range(2):
                xs[r].append(jnp.take_along_axis(placed[r, rows, :], order, axis=1) * g)
        for r in range(2):
            v = times_h(jnp.concatenate(xs[r], axis=0), h2)
            v = butterfly([v[8 * q : 8 * q + 8] for q in range(16)])
            for q in range(16):
                first[r, pl.ds(pl.multiple_of(128 * t + 8 * q, 8), 8), :] = v[q]
        return 0

    def stage_b(t, _):
        rows = [pl.ds(pl.multiple_of(128 * k + 8 * t, 8), 8) for k in range(32)]
        for r in range(2):
            v = butterfly([first[r, rows[k], :] for k in range(32)])
            for k in range(32):
                first[r, rows[k], :] = v[k]
        return 0

    def stage_c(t, _):
        rows = [pl.ds(64 * t + s, 8, stride=8) for s in range(8)]
        ys = [butterfly([first[r, rows[s], :] for s in range(8)]) for r in range(2)]
        for s in range(8):
            scale = gathered[3, rows[s], :] * (1.0 / FEATURE_COUNT)
            phase = gathered[4, rows[s], :]
            for r in range(2):
                feats[r, rows[s], :] = cosine(scale * ys[r][s] + phase)
        return 0

    def stage_d(t, acc):
        out = []
        rows = [pl.ds(pl.multiple_of(128 * t + 8 * q, 8), 8) for q in range(16)]
        weight = [gathered[5, rows[q], :] for q in range(16)]
        for r in range(2):
            v = [feats[r, rows[q], :] * weight[q] for q in range(16)]
            while len(v) > 1:
                v = [v[k] + v[k + 1] for k in range(0, len(v), 2)]
            out.append(acc[r] + v[0])
        return tuple(out)

    to_smem = pltpu.make_async_copy(places_all.reshape(64, 1, LANES), places_ref, own.at[7])
    for step in PLAN:
        if isinstance(step, int):
            advance(groups[step])
        elif step == "order":
            get_perms.wait()
            lax.fori_loop(0, 8, order_of, 0)
        elif step == "t":
            to_smem.start()
            stage_t()
            lax.fori_loop(0, 16, stage_u, 0, unroll=2)
        elif step == "f":
            lax.fori_loop(0, 16, stage_f, 0, unroll=8)
            to_smem.wait()
        else:
            stage, low, high = step
            loop, unroll = {
                "g": (stage_g, 1), "m": (stage_m, 4), "b": (stage_b, 1), "c": (stage_c, 4)
            }[stage]
            lax.fori_loop(low, high, loop, 0, unroll=unroll)

    zero = jnp.zeros((8, LANES), F32)
    acc = lax.fori_loop(0, 32, stage_d, (zero, zero))
    line = jnp.zeros((1, LANES), F32)
    lane = lax.broadcasted_iota(jnp.int32, (1, LANES), 1)
    residual = []
    for r in range(2):
        p = jnp.sum(acc[r], axis=(0, 1), keepdims=True) * (1.0 / math.sqrt(FEATURE_COUNT))
        line = jnp.where(lane == 2 * me + r, p, line)
        residual.append((p - targets_ref[2 * me + r]) * (1.0 / 16.0))
    lines[x, y, z, c] = line

    def gradients(p, core, t):
        out = []
        for i in range(16):
            row = 1024 * t + (i // 4) * 256 + ((i // 2) % 2) * 128 + (i % 2) * 32 + 8 * p + core * 64
            rows = pl.ds(pl.multiple_of(row, 8), 8)
            out.append(feats[0, rows, :] * residual[0] + feats[1, rows, :] * residual[1])
        return out

    for p in range(4):

        def stage_o(t, _, p=p):
            for i, value in enumerate(gradients(p, 1 - c, t)):
                outgoing[p, t, i // 4, (i // 2) % 2, i % 2] = value
            return 0

        lax.fori_loop(0, 4, stage_o, 0, unroll=2)
        sender.start(outgoing.at[p], theirs.at[p], REDUCE_BASE + p, partner)

    reducer = Reducer(place, sender, total)
    whole = {d: ALL for d in "xyzh"}

    def add_theirs(p):
        sender.arrived(theirs.at[p], REDUCE_BASE + p, partner)

        def stage_s(t, _):
            values = gradients(p, c, t)
            values = [v + theirs[p, t, i // 4, (i // 2) % 2, i % 2] for i, v in enumerate(values)]
            for i, value in enumerate(values):
                total[p, t, i // 4, (i // 2) % 2, i % 2] = value
            return 0

        lax.fori_loop(0, 4, stage_s, 0, unroll=2)

    def part_stream(p, order, sem):
        add_theirs(p)
        value = yield from reducer.rings(p, whole, order, slots[3 * p : 3 * p + 3], sem)
        out_ref[8 * p : 8 * p + 8, :] = value

    def last_stream(sem):
        add_theirs(3)
        halves = [
            reducer.rings(3, {**whole, "z": k}, order, slots[9 + 2 * k : 11 + 2 * k], sem + 6 * k)
            for k, order in enumerate((("x", "y"), ("y", "x")))
        ]
        for _ in range(3):
            advance(halves)
            if _ < 2:
                yield
        sel = {**whole, "x": x, "y": y}
        value = yield from reducer.rings(3, sel, ("zz",), slots[13:14], sem + 12)
        out_ref[24:32, :] = value

    sem = REDUCE_BASE + 4
    run_streams(
        [
            part_stream(0, ("x", "y", "zz"), sem),
            part_stream(1, ("y", "zz", "x"), sem + 9),
            part_stream(2, ("zz", "x", "y"), sem + 18),
            last_stream(sem + 27),
            gather_stream(place, sender, REDUCE_BASE + 50, "zyx", get_lines, False),
        ]
    )
    line = jnp.zeros((1, LANES), F32)
    for i in range(64):
        line = line + lines[i // 16, (i // 4) % 4, (i // 2) % 2, i % 2]
    line_ref[...] = line
    sender.finish()


REDUCE_BASE = STREAM_SEMS * (4 * len(GROUPS) + 1)
N_SEMS = REDUCE_BASE + 50 + STREAM_SEMS


def local(
    embeddings,
    sign_flips,
    gaussian,
    scales,
    phases,
    source_blocks,
    block_permutations,
    weights,
    targets,
):
    rows = lambda v: v.reshape(-1, LANES)
    vmem = pl.BlockSpec(memory_space=pltpu.VMEM)
    smem = pl.BlockSpec(memory_space=pltpu.SMEM)
    any_ = pl.BlockSpec(memory_space=pl.ANY)
    field = pltpu.VMEM((2, N_BLOCKS, LANES), F32)
    tiles = lambda *shape: pltpu.VMEM(shape + (8, LANES), F32)
    grad_out, line = pl.pallas_call(
        head_kernel,
        out_shape=(
            jax.ShapeDtypeStruct((32, LANES), F32),
            jax.ShapeDtypeStruct((1, LANES), F32),
        ),
        in_specs=[smem, vmem, vmem] + [any_] * 6,
        out_specs=(vmem, vmem),
        scratch_shapes=[
            pltpu.VMEM((6, 4, 4, 2, 2, 64, LANES), F32),
            pltpu.VMEM((4, 4, 2, 2, 1, LANES), jnp.int32),
            pltpu.SMEM((64, 1, LANES), jnp.int32),
            pltpu.VMEM((64, LANES, LANES), BF16),
            pltpu.VMEM((4, 128, LANES), F32),
            pltpu.VMEM((8, 4, LANES, LANES), F32),
            field, field, field,
            tiles(4, 4, 4, 2, 2), tiles(4, 4, 4, 2, 2), tiles(4, 4, 4, 2, 2),
            pltpu.VMEM((4, 4, 2, 2, 1, LANES), F32),
            pltpu.SemaphoreType.DMA((N_SEMS,)),
            pltpu.SemaphoreType.DMA((N_SEMS,)),
            pltpu.SemaphoreType.DMA((8,)),
            *reduce_scratch(),
        ],
        compiler_params=pltpu.CompilerParams(
            vmem_limit_bytes=60 * 2**20, collective_id=0, has_side_effects=True
        ),
    )(
        targets, source_blocks.reshape(1, -1), embeddings, rows(sign_flips), rows(gaussian),
        rows(scales), rows(phases), rows(weights), block_permutations,
    )

    def hand_over(grad_ref, line_ref, grad_to, line_to):
        grad_to[...] = grad_ref[...]
        line_to[...] = line_ref[...]

    grad_out, line = pl.pallas_call(
        hand_over,
        out_shape=(
            jax.ShapeDtypeStruct((32, LANES), F32),
            jax.ShapeDtypeStruct((1, LANES), F32),
        ),
        in_specs=[vmem, vmem],
        out_specs=(vmem, vmem),
    )(grad_out, line)
    return line.reshape(-1), grad_out.reshape(-1)


def solution(mesh):
    in_specs = (
        P("rows", None), P("feat"), P("feat"), P("feat"), P("feat"), P("feat"),
        P("feat", None, None), P("feat"), P("rows"),
    )
    out_specs = (P("rows"), P(("feat", "rows")))
    return jax.shard_map(local, mesh=mesh, in_specs=in_specs, out_specs=out_specs, check_vma=False)
```

```python
import functools
import math

import jax
import jax.numpy as jnp
from jax import lax
from jax.experimental import pallas as pl
from jax.experimental.pallas import tpu as pltpu
from jax.sharding import PartitionSpec as P

FEATURE_COUNT = 524288
LANES = 128
N_BLOCKS = 4096
F32 = jnp.float32
BF16 = jnp.bfloat16


def signs_128():
    i = lax.broadcasted_iota(jnp.int32, (LANES, LANES), 0)
    j = lax.broadcasted_iota(jnp.int32, (LANES, LANES), 1)
    v = jnp.bitwise_and(i, j)
    v = jnp.bitwise_xor(v, jnp.right_shift(v, 4))
    v = jnp.bitwise_xor(v, jnp.right_shift(v, 2))
    v = jnp.bitwise_xor(v, jnp.right_shift(v, 1))
    return (1 - 2 * jnp.bitwise_and(v, 1)).astype(F32).astype(BF16)


def times_h(x, h2):
    a = x.astype(BF16)
    b = (x - a.astype(F32)).astype(BF16)
    return jnp.dot(jnp.concatenate([a, b], axis=1), h2, preferred_element_type=F32)


def butterfly(values):
    n = len(values)
    half = 1
    values = list(values)
    while half < n:
        out = [None] * n
        for base in range(0, n, 2 * half):
            for k in range(half):
                u, v = values[base + k], values[base + half + k]
                out[base + k] = u + v
                out[base + half + k] = u - v
        values = out
        half *= 2
    return values


def cos_coefficients():
    import numpy as np

    n = 7
    k = np.arange(n)
    u = 0.5 * math.pi**2 * (1.0 + np.cos((k + 0.5) * math.pi / n)) * 1.01
    v = np.stack([u**p for p in range(n)], axis=1)
    c = np.linalg.solve(v, np.cos(np.sqrt(u)))
    return [float(x * (2.0 * math.pi) ** (2 * p)) for p, x in enumerate(c)]


COS = cos_coefficients()


def cosine_of_turns(t):
    r = t - jnp.round(t)
    u = r * r
    acc = COS[-1] * u + COS[-2]
    for c in COS[-3::-1]:
        acc = acc * u + c
    return acc


MESH = pl.DeviceIdType.MESH
ALL = slice(None)
ORDERS = ("yzx", "xzy", "xyz", "yxz")
RELAYED = (2,)
STREAM_SEMS = 14
DIMS = ("x", "y", "zz")


class Place:
    def __init__(self):
        me = lax.axis_index("feat")
        self.h = lax.axis_index("rows")
        self.c = lax.rem(me, 2)
        self.z = lax.rem(me // 2, 2)
        self.y = lax.rem(me // 4, 4)
        self.x = me // 16
        self.zz = 2 * self.h + self.z

    def at(self, x=None, y=None, z=None, c=None, h=None):
        x = self.x if x is None else x
        y = self.y if y is None else y
        z = self.z if z is None else z
        c = self.c if c is None else c
        h = self.h if h is None else h
        return (((x * 4 + y) * 2 + z) * 2 + c, h)

    def along(self, dim, step):
        a = lax.rem(getattr(self, dim) + 4 + step, 4)
        if dim == "zz":
            return self.at(z=lax.rem(a, 2), h=a // 2)
        return self.at(**{dim: a})

    def neighbours(self):
        out = [self.along(d, s) for d in DIMS for s in (1, -1, 2)]
        return out + [self.at(c=1 - self.c)]


def greet(place):
    barrier = pltpu.get_barrier_semaphore()
    others = place.neighbours()
    for device in others:
        pl.semaphore_signal(barrier, inc=1, device_id=device, device_id_type=MESH)
    pl.semaphore_wait(barrier, len(others))


PLAN = (
    0, 2, 3, "order", 1,
    0, 1, 0, 2, 3, 0, 1, 0, 0, "t",
    1, 2, 3, "f", ("g", 0, 32),
    1, ("g", 32, 64),
    2, 1, ("m", 0, 16),
    3, 2, ("m", 16, 32),
    ("b", 0, 16),
    2, 3, ("c", 0, 64), 3,
)


class Sender:
    def __init__(self, send, recv):
        self.send, self.recv = send, recv
        self.started = []

    def copy(self, ref, dst, sem, device):
        return pltpu.make_async_remote_copy(
            src_ref=ref, dst_ref=dst, send_sem=self.send.at[sem], recv_sem=self.recv.at[sem],
            device_id=device, device_id_type=MESH,
        )

    def start(self, ref, dst, sem, device):
        copy = self.copy(ref, dst, sem, device)
        copy.start()
        self.started.append(copy)

    def arrived(self, ref, sem, device):
        self.copy(ref, ref, sem, device).wait_recv()

    def finish(self):
        for copy in self.started:
            copy.wait_send()


def gather_stream(place, sender, base, order, get, halves):
    sel = {"x": place.x, "y": place.y, "z": place.z, "c": place.c}
    partner = place.at(c=1 - place.c)
    sem = base
    mirrored = []

    def mirror(index, **where):
        here = get({**sel, **where}, None)
        sender.start(here, here, index, partner)
        mirrored.append((get({**sel, **where, "c": 1 - place.c}, None), index))

    relays = 0
    for phase, dim in enumerate(order):
        final = phase == 2
        if dim == "z":
            other = 1 - place.z
            ways = ((0, place.h), (1, 1 - place.h)) if halves else ((None, place.h),)
            for k, (half, h) in enumerate(ways):
                ref = get(sel, half)
                sender.start(ref, ref, sem + k, place.at(z=other, h=h))
            if final:
                mirror(base + 10)
            yield
            for k, (half, h) in enumerate(ways):
                sender.arrived(get({**sel, "z": other}, half), sem + k, place.at(z=other, h=h))
            if final:
                mirror(base + 11, z=other)
            sem += 2
        elif halves and phase in RELAYED:
            relays += 1
            a = sel[dim]
            up, down = place.along(dim, 1), place.along(dim, -1)
            below, above, across = (lax.rem(a + k, 4) for k in (3, 1, 2))
            own = get(sel, None)
            sender.start(own, own, sem, up)
            sender.start(own, own, sem + 1, down)
            if final:
                mirror(base + 10)
            yield
            sender.arrived(get({**sel, dim: below}, None), sem, down)
            ref = get({**sel, dim: below}, 0)
            sender.start(ref, ref, sem + 2, up)
            sender.arrived(get({**sel, dim: above}, None), sem + 1, up)
            ref = get({**sel, dim: above}, 1)
            sender.start(ref, ref, sem + 3, down)
            if final:
                mirror(base + 11, **{dim: below})
                mirror(base + 12, **{dim: above})
            yield
            sender.arrived(get({**sel, dim: across}, 0), sem + 2, down)
            sender.arrived(get({**sel, dim: across}, 1), sem + 3, up)
            if final:
                mirror(base + 13, **{dim: across})
            sem += 4
        else:
            a = sel[dim]
            own = get(sel, None)
            for k, step in enumerate((1, -1, 2)):
                sender.start(own, own, sem + k, place.along(dim, step))
            if final:
                mirror(base + 10)
            yield
            for k, step in enumerate((-1, 1, 2)):
                there = lax.rem(a + 4 + step, 4)
                sender.arrived(get({**sel, dim: there}, None), sem + k, place.along(dim, step))
                if final:
                    mirror(base + 11 + k, **{dim: there})
            sem += 3
        sel[dim] = ALL
    yield
    if relays == 0 and RELAYED:
        yield
    for ref, index in mirrored:
        sender.arrived(ref, index, partner)


def run_streams(streams):
    live = list(streams)
    while live:
        left = []
        for s in live:
            try:
                next(s)
                left.append(s)
            except StopIteration:
                pass
        live = left


def advance(streams):
    for s in streams:
        next(s, None)


class Reducer:
    def __init__(self, place, sender, total):
        self.place, self.sender, self.total = place, sender, total

    def entry(self, p, sel, dim, a):
        here = {**sel, "z": lax.rem(a, 2), "h": a // 2} if dim == "zz" else {**sel, dim: a}
        return (p, *(here[d] for d in "xyzh"))

    def start(self, p, sel, dim, slots, sem):
        a = getattr(self.place, dim)
        for k, step in enumerate((1, -1, 2)):
            there = lax.rem(a + 4 + step, 4)
            self.sender.start(
                self.total.at[self.entry(p, sel, dim, there)], slots.at[k], sem + k,
                self.place.along(dim, step),
            )

    def finish(self, p, sel, dim, slots, sem):
        for k, step in enumerate((-1, 1, 2)):
            self.sender.arrived(slots.at[k], sem + k, self.place.along(dim, step))
        i = self.entry(p, sel, dim, getattr(self.place, dim))
        value = (self.total[i] + slots[0]) + (slots[1] + slots[2])
        self.total[i] = value
        return i, value

    def pinned(self, dim):
        if dim == "zz":
            return {"z": self.place.z, "h": self.place.h}
        return {dim: getattr(self.place, dim)}

    def rings(self, p, sel, order, slots, sem):
        for dim, slot in zip(order, slots):
            self.start(p, sel, dim, slot, sem)
            yield
            value = self.finish(p, sel, dim, slot, sem)[1]
            sel = {**sel, **self.pinned(dim)}
            sem += 3
        return value


def reduce_scratch():
    shapes = [(4, 2, 2), (2, 2), (), (4, 2, 2), (4,), (), (4, 4), (4,), ()]
    shapes += [(4, 2), (2,), (4, 2), (2,), ()]
    return [pltpu.VMEM((3,) + shape + (8, LANES), F32) for shape in shapes]


GROUPS = ((0, 1), (1, 3), (3, 5), (5, 6))


def head_kernel(
    targets_ref, sources_ref, emb_ref, signs_ref, gaussian_ref, scales_ref, phases_ref,
    weights_ref, perms_ref,
    out_ref, line_ref,
    gathered7, places_all, places_ref, perms, emb32, part, first, placed, feats,
    outgoing, theirs, total, lines,
    send, recv, own, *slots,
):
    place = Place()
    x, y, z, c, h = place.x, place.y, place.z, place.c, place.h
    partner = place.at(c=1 - c)
    me = ((x * 4 + y) * 2 + z) * 2 + c
    given = [signs_ref, None, gaussian_ref, scales_ref, phases_ref, weights_ref]
    copies = []
    for v, ref in enumerate(given):
        if ref is not None:
            copies.append(pltpu.make_async_copy(ref, gathered7.at[v, x, y, z, c], own.at[v]))
    get_perms = pltpu.make_async_copy(perms_ref, perms, own.at[6])
    for copy in copies:
        copy.start()
    get_perms.start()
    places_all[x, y, z, c, 0:1, 0:64] = sources_ref[...]
    greet(place)
    for copy in copies:
        copy.wait()
    sender = Sender(send, recv)

    def getter(group, quarter):
        vs = slice(*GROUPS[group])

        def get(sel, half):
            rows = pl.ds(16 * quarter, 16) if half is None else pl.ds(16 * quarter + 8 * half, 8)
            return gathered7.at[vs, sel["x"], sel["y"], sel["z"], sel["c"], rows, :]

        return get

    def get_places(sel, half):
        return places_all.at[sel["x"], sel["y"], sel["z"], sel["c"]]

    def get_lines(sel, half):
        return lines.at[sel["x"], sel["y"], sel["z"], sel["c"]]

    groups = []
    for group in range(len(GROUPS)):
        groups.append([])
        for q in range(4):
            base = STREAM_SEMS * (4 * group + q)
            groups[group].append(
                gather_stream(place, sender, base, ORDERS[q], getter(group, q), True)
            )
    groups[0].append(gather_stream(place, sender, STREAM_SEMS * 4 * len(GROUPS), "zyx", get_places, False))

    lanes = lax.broadcasted_iota(jnp.int32, (8, LANES), 1).astype(F32).astype(BF16)

    gathered = gathered7.reshape(6, N_BLOCKS, LANES)

    h1 = signs_128()
    h2 = jnp.concatenate([h1, h1], axis=0)
    for d in range(4):
        emb32[d] = emb_ref[:, d * LANES : (d + 1) * LANES].astype(F32)
    emb = [[emb32[d, pl.ds(2 * me + r, 1), :] for d in range(4)] for r in range(2)]

    def order_of(t, _):
        rows = []
        for q in range(8):
            line = lax.dot_general(
                lanes, perms[8 * t + q], (((1,), (1,)), ((), ())), preferred_element_type=F32
            )
            rows.append(line[0:1])
        gathered7[1, x, y, z, c, pl.ds(pl.multiple_of(8 * t, 8), 8), :] = jnp.concatenate(rows, axis=0)
        return 0

    def stage_t():
        for k_hi in range(8):
            for d in range(4):
                s = gathered[0, pl.ds(512 * k_hi + d, LANES, stride=4), :]
                part[k_hi, d] = jnp.dot(h1, s.astype(BF16), preferred_element_type=F32)

    def stage_u(t, _):
        rows = pl.ds(pl.multiple_of(8 * t, 8), 8)
        cols = []
        for d in range(4):
            cols.append(butterfly([part[k, d, rows, :] for k in range(8)]))
        for k in range(8):
            for r in range(2):
                u = butterfly([emb[r][d] * cols[d][k] for d in range(4)])
                for b in range(4):
                    placed[r, pl.ds(512 * k + 32 * t + b, 8, stride=4), :] = u[b]
        return 0

    def stage_f(t, _):
        rows = pl.ds(pl.multiple_of(256 * t, 256), 256)
        for r in range(2):
            first[r, rows, :] = times_h(placed[r, rows, :], h2)
        return 0

    def stage_g(t, _):
        for q in range(64):
            s = places_ref[t, 0, q]
            for r in range(2):
                placed[r, pl.ds(64 * t + q, 1), :] = first[r, pl.ds(s, 1), :]
        return 0

    def stage_m(t, _):
        xs = [[], []]
        for q in range(16):
            rows = pl.ds(pl.multiple_of(128 * t + 8 * q, 8), 8)
            order = gathered[1, rows, :].astype(jnp.int32)
            g = gathered[2, rows, :]
            for r in range(2):
                xs[r].append(jnp.take_along_axis(placed[r, rows, :], order, axis=1) * g)
        for r in range(2):
            v = times_h(jnp.concatenate(xs[r], axis=0), h2)
            v = butterfly([v[8 * q : 8 * q + 8] for q in range(16)])
            for q in range(16):
                first[r, pl.ds(pl.multiple_of(128 * t + 8 * q, 8), 8), :] = v[q]
        return 0

    def stage_b(t, _):
        rows = [pl.ds(pl.multiple_of(128 * k + 8 * t, 8), 8) for k in range(32)]
        for r in range(2):
            v = butterfly([first[r, rows[k], :] for k in range(32)])
            for k in range(32):
                first[r, rows[k], :] = v[k]
        return 0

    def stage_c(t, _):
        rows = [pl.ds(64 * t + s, 8, stride=8) for s in range(8)]
        ys = [butterfly([first[r, rows[s], :] for s in range(8)]) for r in range(2)]
        for s in range(8):
            scale = gathered[3, rows[s], :] * (1.0 / (2.0 * math.pi * FEATURE_COUNT))
            phase = gathered[4, rows[s], :] * (1.0 / (2.0 * math.pi))
            for r in range(2):
                feats[r, rows[s], :] = cosine_of_turns(scale * ys[r][s] + phase)
        return 0

    def stage_d(t, acc):
        out = []
        rows = [pl.ds(pl.multiple_of(128 * t + 8 * q, 8), 8) for q in range(16)]
        weight = [gathered[5, rows[q], :] for q in range(16)]
        for r in range(2):
            v = [feats[r, rows[q], :] * weight[q] for q in range(16)]
            while len(v) > 1:
                v = [v[k] + v[k + 1] for k in range(0, len(v), 2)]
            out.append(acc[r] + v[0])
        return tuple(out)

    to_smem = pltpu.make_async_copy(places_all.reshape(64, 1, LANES), places_ref, own.at[7])
    for step in PLAN:
        if isinstance(step, int):
            advance(groups[step])
        elif step == "order":
            get_perms.wait()
            lax.fori_loop(0, 8, order_of, 0)
        elif step == "t":
            to_smem.start()
            stage_t()
            lax.fori_loop(0, 16, stage_u, 0, unroll=2)
        elif step == "f":
            lax.fori_loop(0, 16, stage_f, 0, unroll=8)
            to_smem.wait()
        else:
            stage, low, high = step
            loop, unroll = {
                "g": (stage_g, 1), "m": (stage_m, 8), "b": (stage_b, 1), "c": (stage_c, 8)
            }[stage]
            lax.fori_loop(low, high, loop, 0, unroll=unroll)

    zero = jnp.zeros((8, LANES), F32)
    acc = lax.fori_loop(0, 32, stage_d, (zero, zero))
    line = jnp.zeros((1, LANES), F32)
    lane = lax.broadcasted_iota(jnp.int32, (1, LANES), 1)
    residual = []
    for r in range(2):
        p = jnp.sum(acc[r], axis=(0, 1), keepdims=True) * (1.0 / math.sqrt(FEATURE_COUNT))
        line = jnp.where(lane == 2 * me + r, p, line)
        residual.append((p - targets_ref[2 * me + r]) * (1.0 / 16.0))
    lines[x, y, z, c] = line
    line_stream = gather_stream(place, sender, REDUCE_BASE + 50, "zyx", get_lines, False)
    next(line_stream)

    def gradients(p, core, t):
        out = []
        for i in range(16):
            row = 1024 * t + (i // 4) * 256 + ((i // 2) % 2) * 128 + (i % 2) * 32 + 8 * p + core * 64
            rows = pl.ds(pl.multiple_of(row, 8), 8)
            out.append(feats[0, rows, :] * residual[0] + feats[1, rows, :] * residual[1])
        return out

    for p in range(4):

        def stage_o(t, _, p=p):
            for i, value in enumerate(gradients(p, 1 - c, t)):
                outgoing[p, t, i // 4, (i // 2) % 2, i % 2] = value
            return 0

        lax.fori_loop(0, 4, stage_o, 0, unroll=2)
        sender.start(outgoing.at[p], theirs.at[p], REDUCE_BASE + p, partner)

    reducer = Reducer(place, sender, total)
    whole = {d: ALL for d in "xyzh"}

    def add_theirs(p):
        sender.arrived(theirs.at[p], REDUCE_BASE + p, partner)

        def stage_s(t, _):
            values = gradients(p, c, t)
            values = [v + theirs[p, t, i // 4, (i // 2) % 2, i % 2] for i, v in enumerate(values)]
            for i, value in enumerate(values):
                total[p, t, i // 4, (i // 2) % 2, i % 2] = value
            return 0

        lax.fori_loop(0, 4, stage_s, 0, unroll=2)

    def part_stream(p, order, sem):
        add_theirs(p)
        value = yield from reducer.rings(p, whole, order, slots[3 * p : 3 * p + 3], sem)
        out_ref[8 * p : 8 * p + 8, :] = value

    def last_stream(sem):
        add_theirs(3)
        halves = [
            reducer.rings(3, {**whole, "z": k}, order, slots[9 + 2 * k : 11 + 2 * k], sem + 6 * k)
            for k, order in enumerate((("x", "y"), ("y", "x")))
        ]
        for _ in range(3):
            advance(halves)
            if _ < 2:
                yield
        sel = {**whole, "x": x, "y": y}
        value = yield from reducer.rings(3, sel, ("zz",), slots[13:14], sem + 12)
        out_ref[24:32, :] = value

    sem = REDUCE_BASE + 4
    run_streams(
        [
            part_stream(0, ("x", "y", "zz"), sem),
            part_stream(1, ("y", "zz", "x"), sem + 9),
            part_stream(2, ("zz", "x", "y"), sem + 18),
            last_stream(sem + 27),
            line_stream,
        ]
    )
    line = jnp.zeros((1, LANES), F32)
    for i in range(64):
        line = line + lines[i // 16, (i // 4) % 4, (i // 2) % 2, i % 2]
    line_ref[...] = line
    sender.finish()


REDUCE_BASE = STREAM_SEMS * (4 * len(GROUPS) + 1)
N_SEMS = REDUCE_BASE + 50 + STREAM_SEMS


def local(
    embeddings,
    sign_flips,
    gaussian,
    scales,
    phases,
    source_blocks,
    block_permutations,
    weights,
    targets,
):
    rows = lambda v: v.reshape(-1, LANES)
    vmem = pl.BlockSpec(memory_space=pltpu.VMEM)
    smem = pl.BlockSpec(memory_space=pltpu.SMEM)
    any_ = pl.BlockSpec(memory_space=pl.ANY)
    field = pltpu.VMEM((2, N_BLOCKS, LANES), F32)
    tiles = lambda *shape: pltpu.VMEM(shape + (8, LANES), F32)
    grad_out, line = pl.pallas_call(
        head_kernel,
        out_shape=(
            jax.ShapeDtypeStruct((32, LANES), F32),
            jax.ShapeDtypeStruct((1, LANES), F32),
        ),
        in_specs=[smem, vmem, vmem] + [any_] * 6,
        out_specs=(vmem, vmem),
        scratch_shapes=[
            pltpu.VMEM((6, 4, 4, 2, 2, 64, LANES), F32),
            pltpu.VMEM((4, 4, 2, 2, 1, LANES), jnp.int32),
            pltpu.SMEM((64, 1, LANES), jnp.int32),
            pltpu.VMEM((64, LANES, LANES), BF16),
            pltpu.VMEM((4, 128, LANES), F32),
            pltpu.VMEM((8, 4, LANES, LANES), F32),
            field, field, field,
            tiles(4, 4, 4, 2, 2), tiles(4, 4, 4, 2, 2), tiles(4, 4, 4, 2, 2),
            pltpu.VMEM((4, 4, 2, 2, 1, LANES), F32),
            pltpu.SemaphoreType.DMA((N_SEMS,)),
            pltpu.SemaphoreType.DMA((N_SEMS,)),
            pltpu.SemaphoreType.DMA((8,)),
            *reduce_scratch(),
        ],
        compiler_params=pltpu.CompilerParams(
            vmem_limit_bytes=60 * 2**20, collective_id=0, has_side_effects=True
        ),
    )(
        targets, source_blocks.reshape(1, -1), embeddings, rows(sign_flips), rows(gaussian),
        rows(scales), rows(phases), rows(weights), block_permutations,
    )

    def hand_over(grad_ref, line_ref, grad_to, line_to):
        grad_to[...] = grad_ref[...]
        line_to[...] = line_ref[...]

    grad_out, line = pl.pallas_call(
        hand_over,
        out_shape=(
            jax.ShapeDtypeStruct((32, LANES), F32),
            jax.ShapeDtypeStruct((1, LANES), F32),
        ),
        in_specs=[vmem, vmem],
        out_specs=(vmem, vmem),
    )(grad_out, line)
    return line.reshape(-1), grad_out.reshape(-1)


def solution(mesh):
    in_specs = (
        P("rows", None), P("feat"), P("feat"), P("feat"), P("feat"), P("feat"),
        P("feat", None, None), P("feat"), P("rows"),
    )
    out_specs = (P("rows"), P(("feat", "rows")))
    return jax.shard_map(local, mesh=mesh, in_specs=in_specs, out_specs=out_specs, check_vma=False)
```
